512 devices in a mesh: dp: 32 (over y, x, core), ctx: 16 (over z).
Axes of the slice: x: 4, y: 4, z: 16, core: 2. Of those that a mesh axis runs over, the one named last changes fastest.
Arguments:
- layer_input: bfloat16 [32, 2048, 1024], P('dp', 'ctx'), may hold values from -6 to 6
- projected: bfloat16 [32, 2048, 3072], P('dp', 'ctx'), may hold values from -6 to 6
- grad_output: bfloat16 [32, 2048, 1024], P('dp', 'ctx'), may hold values from -12 to 12
- w_qkv: bfloat16 [1024, 3072], P('dp', 'ctx'), may hold values from -0.1875 to 0.1875
- lengths: int32 [32, 8], P('dp'), may hold values from 1 to 1024, 2048 in all within a row
- block_perm: int32 [32, 16], P('dp'), may hold values from 0 to 15, each once within a row
Outputs:
- grad_input: bfloat16 [32, 2048, 1024], P('dp', 'ctx')
- grad_weight: float32 [1024, 3072], P('dp', 'ctx')
The draws below stay inside these ranges and needn't reach their ends.
Inputs may be any that keep to these rules, and one draw needn't show every extreme that they name: Every row of lengths sums to 2048 and has an entry equal to 1024. Every row of block_perm names each of the 16 blocks once; slot block s holds packed positions block_perm[g, s] * 128 to block_perm[g, s] * 128 + 127.
All inputs are finite; a program needn't handle non-finite values.
Results may differ from the reference program's by a relative error of at most 0.0065.
Values may be sent and summed in bfloat16 or wider, within the bound.
A program may use at most 64 MiB of HBM per device.

```python
import math
import jax
import jax.numpy as jnp
import numpy as np
from jax import lax

D = 1024
HEADS = 16
DH = 64
BLK = 128
USERS = 8
CTX_TOK = 2048
MAXLEN = 1024
NBLK = 16
GROUPS = 32
N_CTX = 16


def spiked(array, stream_key, source, target, blocks, factor):
    owner, partner = [(jnp.arange(array.shape[dim]) // (array.shape[dim] // blocks)).reshape([-1 if axis == dim else 1 for axis in range(array.ndim)]) for dim in (source, target)]
    chosen = jax.random.permutation(stream_key, blocks)[partner]
    strong = (owner == chosen) | (owner == (partner + blocks // 2) % blocks)
    return jnp.where(strong, factor * array, array)


def block_levels(own_key, extent, cuts, low, largest):
    level, own = 1.0, jax.random.fold_in(own_key, 6)
    for axis_at, blocks in cuts:
        draws = jnp.exp(jax.random.uniform(jax.random.fold_in(own, axis_at), (blocks,), jnp.float32, low / len(cuts), largest / len(cuts)))
        level = level * jnp.repeat(draws, extent[axis_at] // blocks).reshape([-1 if axis == axis_at else 1 for axis in range(len(extent))])
    return level


def length_profile(count, total, limit, lean):
    portions = [(1 << 20) // math.isqrt(rank ** lean) + 1 for rank in range(2, count + 1)]
    surplus, counts = total - limit - (count - 1), [1] * (count - 1)
    while surplus > 0:
        free = [i for i in range(count - 1) if counts[i] < limit]
        pool, left = sum([portions[i] for i in free]), surplus
        for i in free:
            addition = min(limit - counts[i], max(1, left * portions[i] // pool), surplus)
            counts[i] = counts[i] + addition
            surplus = surplus - addition
    return np.array([limit] + counts)


def ragged_sizes(rng, count, total, bound, lean):
    if count == 2:
        one = jax.random.randint(rng, (), max(1, total - bound), min(bound, total - 1) + 1)
        return jnp.stack([one, total - one])
    sizes = jnp.asarray(length_profile(count, total, bound, lean), jnp.int32)
    twos = (count - 1) // 2
    giver, sink = sizes[1:1 + 2 * twos:2], sizes[2:2 + 2 * twos:2]
    margin = jnp.minimum(giver - 1, bound - sink)
    shifted = jax.random.randint(jax.random.fold_in(rng, 1), (twos,), 0, 1 << 20) % (margin + 1)
    sizes = sizes.at[1:1 + 2 * twos:2].set(giver - shifted).at[2:2 + 2 * twos:2].set(sink + shifted)
    return sizes[jax.random.permutation(jax.random.fold_in(rng, 2), count)]


def noise(own_key, shape, deviation, limit, split=(), kind=jnp.bfloat16):
    factor_of = block_levels(own_key, shape, split, -0.22, 0.18) if split else 1.0
    entries = jax.random.normal(own_key, shape, jnp.float32) * deviation * factor_of
    return jnp.minimum(jnp.maximum(entries, -limit), limit).astype(kind)


def bell_draw_with(key, shape, scale, limit, cuts, heavy, held_as=jnp.bfloat16):
    drawn = scale * jax.random.normal(key, shape, jnp.float32)
    if cuts:
        drawn = drawn * block_levels(key, shape, cuts, -0.22, 0.18)
    return jnp.clip(spiked(drawn, jax.random.fold_in(key, 3), *heavy), -limit, limit).astype(held_as)


def setup_inputs(seed: int = 0) -> dict:
    arg_keys = jax.random.split(jax.random.key(seed), 7)
    layer_input = bell_draw_with(arg_keys[0], (GROUPS, CTX_TOK, D), 1.0, 6.0, ((0, 32), (1, 16)), (0, 2, 32, 2.75))
    projected = noise(arg_keys[1], (GROUPS, CTX_TOK, 3 * D), 1.0, 6.0, ((0, 32), (1, 16)))
    grad_output = noise(arg_keys[2], (GROUPS, CTX_TOK, D), 2.0, 12.0, ((0, 32), (1, 16)))
    w_qkv = noise(arg_keys[3], (D, 3 * D), D ** -0.5, 0.1875, ((0, 32), (1, 16)))
    lengths = jax.vmap(lambda own: ragged_sizes(own, USERS, CTX_TOK, MAXLEN, 2))(jax.random.split(arg_keys[4], GROUPS)).reshape((GROUPS, USERS)).astype(jnp.int32)
    block_perm = jax.vmap(lambda own: jax.random.permutation(own, NBLK))(jax.random.split(arg_keys[5], GROUPS)).reshape((GROUPS, NBLK)).astype(jnp.int32)
    return {"layer_input": layer_input, "projected": projected, "grad_output": grad_output, "w_qkv": w_qkv, "lengths": lengths, "block_perm": block_perm}


def silu_slope(value):
    sigma = jax.nn.sigmoid(value)
    return sigma * (1.0 + value * (1.0 - sigma))

def row_layout(user_lengths, slot_blocks):
    slots = jnp.arange(CTX_TOK, dtype=jnp.int32)
    position = slot_blocks[slots // BLK] * BLK + slots % BLK
    ends = jnp.cumsum(user_lengths).astype(jnp.int32)
    segment = lax.optimization_barrier(jnp.sum((position[:, None] >= ends[None, :]).astype(jnp.int32), axis=1))
    member = segment[:, None] == jnp.arange(USERS, dtype=jnp.int32)[None, :]
    user_len = lax.optimization_barrier(jnp.sum(jnp.where(member, user_lengths[None, :], 0), axis=1))
    row_scale = lax.rsqrt(user_len.astype(jnp.float32))
    return (position, segment, row_scale)

def head_backward(pre_head, grad_head, position, segment, row_scale):
    active = jax.nn.silu(pre_head.astype(jnp.float32)).astype(jnp.bfloat16)
    queries = active[:, 0]
    key_rows = active[:, 1]
    value_rows = active[:, 2]
    scale = DH ** (-0.5)
    scores = jnp.dot(queries, key_rows.T, preferred_element_type=jnp.float32) * scale
    visible = (segment[:, None] == segment[None, :]) & (position[None, :] <= position[:, None])
    sigma = jax.nn.sigmoid(scores)
    weights = jnp.where(visible, scores * sigma * row_scale[:, None], 0.0).astype(jnp.bfloat16)
    grad_weights = jnp.dot(grad_head, value_rows.T, preferred_element_type=jnp.float32)
    slope = grad_weights * sigma * (1.0 + scores * (1.0 - sigma)) * (row_scale[:, None] * scale)
    grad_scores = jnp.where(visible, slope, 0.0).astype(jnp.bfloat16)
    grad_query = jnp.dot(grad_scores, key_rows, preferred_element_type=jnp.float32)
    grad_key = jnp.dot(grad_scores.T, queries, preferred_element_type=jnp.float32)
    grad_value = jnp.dot(weights.T, grad_head, preferred_element_type=jnp.float32)
    grads = jnp.stack([grad_query, grad_key, grad_value], axis=1)
    return (grads * silu_slope(pre_head.astype(jnp.float32))).astype(jnp.bfloat16)

def input_gradient(grad_pre, weight):
    group_cols = 3 * D // N_CTX
    pre_groups = grad_pre.reshape(CTX_TOK, N_CTX, group_cols).transpose(1, 0, 2)
    weight_groups = weight.reshape(D, N_CTX, group_cols).transpose(1, 0, 2)

    def add_group(total, item):
        term = jnp.dot(item[0], item[1].T, preferred_element_type=jnp.float32).astype(jnp.bfloat16)
        return (total + lax.optimization_barrier(term).astype(jnp.float32), None)
    total, unused = lax.scan(add_group, jnp.zeros((CTX_TOK, D), jnp.float32), (pre_groups, weight_groups))
    return total.astype(jnp.bfloat16)

def reference(layer_input, projected, grad_output, w_qkv, lengths, block_perm):

    def one_group(weight_total, group_item):
        tokens, pre_group, grad_group, user_lengths, slot_blocks = group_item
        position, segment, row_scale = row_layout(user_lengths, slot_blocks)
        pre_heads = pre_group.reshape(CTX_TOK, HEADS, 3, DH).transpose(1, 0, 2, 3)
        grad_heads = grad_group.reshape(CTX_TOK, HEADS, DH).transpose(1, 0, 2)

        def per_head(operands):
            return head_backward(operands[0], operands[1], position, segment, row_scale)
        head_grads = lax.map(per_head, (pre_heads, grad_heads))
        grad_pre = head_grads.transpose(1, 0, 2, 3).reshape(CTX_TOK, 3 * D)
        grad_rows = input_gradient(grad_pre, w_qkv)
        weight_total = weight_total + jnp.dot(tokens.T, grad_pre, preferred_element_type=jnp.float32)
        return (weight_total, grad_rows)
    weight_total, grad_input = lax.scan(one_group, jnp.zeros((D, 3 * D), jnp.float32), (layer_input, projected, grad_output, lengths, block_perm))
    return (grad_input, weight_total * (1.0 / GROUPS))
```

```python
import functools

import jax
import jax.numpy as jnp
from jax import lax
from jax.experimental import pallas as pl
from jax.experimental.pallas import tpu as pltpu
from jax.sharding import PartitionSpec as P

DH = 64
BLK = 128
MESH = pl.DeviceIdType.MESH
VMEM = pl.BlockSpec(memory_space=pltpu.VMEM)


def attention_kernel(tile, lengths_ref, perm_ref, x_ref, out_ref, q_s, k_s, v_s, g_s, kt_s, gq_s, gk_s, gv_s, start_s, scale_s):
    slots = x_ref.shape[0]
    whole = slots * BLK
    users = lengths_ref.shape[1]
    count = whole // tile

    pos = lax.broadcasted_iota(jnp.int32, (count, tile), 0) * tile + lax.broadcasted_iota(jnp.int32, (count, tile), 1)
    first = jnp.zeros((count, tile), jnp.int32)
    length = jnp.ones((count, tile), jnp.int32)
    end = jnp.int32(0)
    for user in range(users):
        begin = end
        end = begin + lengths_ref[0, user]
        inside = pos >= begin
        first = jnp.where(inside, begin, first)
        length = jnp.where(inside, lengths_ref[0, user], length)
    start_s[...] = first
    scale_s[...] = lax.rsqrt(length.astype(jnp.float32))

    @pl.loop(0, slots)
    def _(slot):
        row = pl.multiple_of(perm_ref[0, slot] * BLK, BLK)
        block = x_ref[slot]
        pre = block[:, : 3 * DH].astype(jnp.float32)
        active = (pre * jax.nn.sigmoid(pre)).astype(jnp.bfloat16)
        q_s[pl.ds(row, BLK), :] = active[:, :DH] * jnp.bfloat16(0.0625)
        key = active[:, DH : 2 * DH]
        k_s[pl.ds(row, BLK), :] = key
        kt_s[:, pl.ds(row, BLK)] = key.T
        v_s[pl.ds(row, BLK), :] = active[:, 2 * DH :]
        g_s[pl.ds(row, BLK), :] = block[:, 3 * DH :]

    gq_s[...] = jnp.zeros_like(gq_s)
    contract = (((1,), (1,)), ((), ()))

    @pl.loop(0, count)
    def _(key_block):
        key_row = pl.multiple_of(key_block * tile, tile)
        last_key = key_row + tile - 1
        limit = jnp.int32(0)
        total = jnp.int32(0)
        for user in range(users):
            begin = total
            total = begin + lengths_ref[0, user]
            limit = jnp.where(last_key >= begin, total, limit)
        stop = (limit + tile - 1) // tile
        keys = k_s[pl.ds(key_row, tile), :]
        values = v_s[pl.ds(key_row, tile), :]
        keys_t = kt_s[:, pl.ds(key_row, tile)]
        key_pos = key_row + lax.broadcasted_iota(jnp.int32, (tile, 1), 0)

        def step(query_block, carry):
            gk, gv = carry
            query_row = pl.multiple_of(query_block * tile, tile)
            queries = q_s[pl.ds(query_row, tile), :]
            grads = g_s[pl.ds(query_row, tile), :]
            half = lax.dot_general(keys, queries, contract, preferred_element_type=jnp.float32)
            gw = lax.dot_general(values, grads, contract, preferred_element_type=jnp.float32)
            first_row = start_s[pl.ds(query_block, 1), :]
            scale_row = scale_s[pl.ds(query_block, 1), :]
            query_pos = query_row + lax.broadcasted_iota(jnp.int32, (1, tile), 1)
            visible = (key_pos >= first_row) & (key_pos <= query_pos)
            th = jnp.tanh(half)
            up = 1.0 + th
            w = half * up
            slope = up + w * (1.0 - th)
            weights = jnp.where(visible, w * scale_row, 0.0).astype(jnp.bfloat16)
            gs = jnp.where(visible, gw * slope * scale_row, 0.0).astype(jnp.bfloat16)
            gv = gv + jnp.dot(weights, grads, preferred_element_type=jnp.float32)
            gk = gk + jnp.dot(gs, queries, preferred_element_type=jnp.float32)
            gq_s[:, pl.ds(query_row, tile)] += jnp.dot(keys_t, gs, preferred_element_type=jnp.float32)
            return gk, gv

        zero = jnp.zeros((tile, DH), jnp.float32)
        gk, gv = lax.fori_loop(key_block, stop, step, (zero, zero))
        gk_s[pl.ds(key_row, tile), :] = gk
        gv_s[pl.ds(key_row, tile), :] = gv

    @pl.loop(0, slots)
    def _(slot):
        row = pl.multiple_of(perm_ref[0, slot] * BLK, BLK)
        pre = x_ref[slot][:, : 3 * DH].astype(jnp.float32)
        sigma = jax.nn.sigmoid(pre)
        slope = sigma * (1.0 + pre * (1.0 - sigma))
        gq = gq_s[:, pl.ds(row, BLK)].T * 0.0625
        gk = gk_s[pl.ds(row, BLK), :]
        gv = gv_s[pl.ds(row, BLK), :]
        out_ref[slot, :DH, :] = (gq * slope[:, :DH]).T.astype(jnp.bfloat16)
        out_ref[slot, DH : 2 * DH, :] = (gk * slope[:, DH : 2 * DH]).T.astype(jnp.bfloat16)
        out_ref[slot, 2 * DH :, :] = (gv * slope[:, 2 * DH :]).T.astype(jnp.bfloat16)


def attention(packed, lengths, perm, tile=256):
    slots = packed.shape[0]
    whole = slots * BLK
    vmem = pl.BlockSpec(memory_space=pltpu.VMEM)
    smem = pl.BlockSpec(memory_space=pltpu.SMEM)
    bf, f32 = jnp.bfloat16, jnp.float32
    return pl.pallas_call(
        functools.partial(attention_kernel, tile),
        out_shape=jax.ShapeDtypeStruct((slots, 3 * DH, BLK), bf),
        in_specs=[smem, smem, vmem],
        out_specs=vmem,
        scratch_shapes=[
            pltpu.VMEM((whole, DH), bf),
            pltpu.VMEM((whole, DH), bf),
            pltpu.VMEM((whole, DH), bf),
            pltpu.VMEM((whole, DH), bf),
            pltpu.VMEM((DH, whole), bf),
            pltpu.VMEM((DH, whole), f32),
            pltpu.VMEM((whole, DH), f32),
            pltpu.VMEM((whole, DH), f32),
            pltpu.VMEM((whole // tile, tile), jnp.int32),
            pltpu.VMEM((whole // tile, tile), f32),
        ],
        compiler_params=pltpu.CompilerParams(vmem_limit_bytes=32 << 20),
    )(lengths, perm, packed)


def exchange_kernel(n, src_ref, dst_ref, send_sem, recv_sem, local_sem):
    me = lax.axis_index("ctx")
    barrier = pltpu.get_barrier_semaphore()
    for step in range(1, n):
        peer = lax.rem(me + step, n)
        pl.semaphore_signal(barrier, inc=1, device_id={"ctx": peer}, device_id_type=MESH)
    own = pltpu.make_async_copy(src_ref.at[me], dst_ref.at[me], local_sem)
    own.start()
    pl.semaphore_wait(barrier, n - 1)
    copies = []
    for near in range(1, n // 2 + 1):
        for step in sorted({near, n - near}):
            peer = lax.rem(me + step, n)
            copy = pltpu.make_async_remote_copy(
                src_ref=src_ref.at[peer],
                dst_ref=dst_ref.at[me],
                send_sem=send_sem.at[step],
                recv_sem=recv_sem.at[step],
                device_id={"ctx": peer},
                device_id_type=MESH,
            )
            copy.start()
            copies.append(copy)
    own.wait()
    for copy in copies:
        copy.wait()


def exchange(blocks, collective_id):
    n = blocks.shape[0]
    return pl.pallas_call(
        functools.partial(exchange_kernel, n),
        out_shape=jax.ShapeDtypeStruct(blocks.shape, blocks.dtype),
        in_specs=[VMEM],
        out_specs=VMEM,
        scratch_shapes=[
            pltpu.SemaphoreType.DMA((n,)),
            pltpu.SemaphoreType.DMA((n,)),
            pltpu.SemaphoreType.DMA,
        ],
        compiler_params=pltpu.CompilerParams(
            collective_id=collective_id, has_side_effects=True, vmem_limit_bytes=16 << 20
        ),
    )(blocks)


def body(layer_input, projected, grad_output, w_qkv, lengths, block_perm):
    tokens_dev = layer_input.shape[1]
    width = layer_input.shape[2]
    ctx_count = lax.axis_size("ctx")
    data_count = lax.axis_size("dp")
    whole = tokens_dev * ctx_count
    columns = 3 * DH
    packed = jnp.concatenate(
        [
            projected[0].reshape(tokens_dev, ctx_count, columns),
            grad_output[0].reshape(tokens_dev, ctx_count, DH),
        ],
        axis=2,
    ).transpose(1, 0, 2)
    grad_t = attention(exchange(packed, 1), lengths, block_perm)
    tokens = lax.all_gather(layer_input, "ctx", axis=1, tiled=True)[0]
    flat_t = grad_t.transpose(1, 0, 2).reshape(columns, whole)
    weight_local = lax.dot_general(
        tokens, flat_t, (((0,), (1,)), ((), ())), preferred_element_type=jnp.float32
    )
    grad_weight = lax.psum_scatter(weight_local, "dp", scatter_dimension=0, tiled=True) * (
        1.0 / data_count
    )
    back_t = exchange(grad_t, 2).reshape(ctx_count * columns, tokens_dev)
    w_rows = lax.all_gather(w_qkv, "ctx", axis=1, tiled=True)
    w_all = lax.all_gather(w_rows, "dp", axis=0, tiled=True)
    grad_input = lax.dot_general(
        back_t, w_all, (((0,), (1,)), ((), ())), preferred_element_type=jnp.float32
    ).astype(jnp.bfloat16)
    return (grad_input[None], grad_weight)


def solution(mesh):
    return jax.shard_map(
        body,
        mesh=mesh,
        in_specs=(
            P("dp", "ctx", None),
            P("dp", "ctx", None),
            P("dp", "ctx", None),
            P("dp", "ctx"),
            P("dp", None),
            P("dp", None),
        ),
        out_specs=(P("dp", "ctx", None), P("dp", "ctx")),
        check_vma=False,
    )
```

```python
import functools

import jax
import jax.numpy as jnp
from jax import lax
from jax.experimental import pallas as pl
from jax.experimental.pallas import tpu as pltpu
from jax.sharding import PartitionSpec as P

DH = 64
BLK = 128
MESH = pl.DeviceIdType.MESH
VMEM = pl.BlockSpec(memory_space=pltpu.VMEM)
ANY = pl.BlockSpec(memory_space=pl.ANY)


def attention_kernel(tile, lengths_ref, perm_ref, x_ref, out_ref, q_s, k_s, v_s, g_s, kt_s, gq_s, gk_s, gv_s, start_s, scale_s):
    slots = x_ref.shape[0]
    whole = slots * BLK
    users = lengths_ref.shape[1]
    count = whole // tile

    pos = lax.broadcasted_iota(jnp.int32, (count, tile), 0) * tile + lax.broadcasted_iota(jnp.int32, (count, tile), 1)
    first = jnp.zeros((count, tile), jnp.int32)
    length = jnp.ones((count, tile), jnp.int32)
    end = jnp.int32(0)
    for user in range(users):
        begin = end
        end = begin + lengths_ref[0, user]
        inside = pos >= begin
        first = jnp.where(inside, begin, first)
        length = jnp.where(inside, lengths_ref[0, user], length)
    start_s[...] = first
    scale_s[...] = lax.rsqrt(length.astype(jnp.float32))

    @pl.loop(0, slots)
    def _(slot):
        row = pl.multiple_of(perm_ref[0, slot] * BLK, BLK)
        block = x_ref[slot]
        pre = block[:, : 3 * DH].astype(jnp.float32)
        active = (pre * jax.nn.sigmoid(pre)).astype(jnp.bfloat16)
        q_s[pl.ds(row, BLK), :] = active[:, :DH] * jnp.bfloat16(0.0625)
        key = active[:, DH : 2 * DH]
        k_s[pl.ds(row, BLK), :] = key
        kt_s[:, pl.ds(row, BLK)] = key.T
        v_s[pl.ds(row, BLK), :] = active[:, 2 * DH :]
        g_s[pl.ds(row, BLK), :] = block[:, 3 * DH :]

    gq_s[...] = jnp.zeros_like(gq_s)
    contract = (((1,), (1,)), ((), ()))

    @pl.loop(0, count)
    def _(key_block):
        key_row = pl.multiple_of(key_block * tile, tile)
        last_key = key_row + tile - 1
        limit = jnp.int32(0)
        total = jnp.int32(0)
        for user in range(users):
            begin = total
            total = begin + lengths_ref[0, user]
            limit = jnp.where(last_key >= begin, total, limit)
        stop = (limit + tile - 1) // tile
        keys = k_s[pl.ds(key_row, tile), :]
        values = v_s[pl.ds(key_row, tile), :]
        keys_t = kt_s[:, pl.ds(key_row, tile)]
        key_pos = key_row + lax.broadcasted_iota(jnp.int32, (tile, 1), 0)

        def step(query_block, carry):
            gk, gv = carry
            query_row = pl.multiple_of(query_block * tile, tile)
            queries = q_s[pl.ds(query_row, tile), :]
            grads = g_s[pl.ds(query_row, tile), :]
            half = lax.dot_general(keys, queries, contract, preferred_element_type=jnp.float32)
            gw = lax.dot_general(values, grads, contract, preferred_element_type=jnp.float32)
            first_row = start_s[pl.ds(query_block, 1), :]
            scale_row = scale_s[pl.ds(query_block, 1), :]
            query_pos = query_row + lax.broadcasted_iota(jnp.int32, (1, tile), 1)
            visible = (key_pos >= first_row) & (key_pos <= query_pos)
            th = jnp.tanh(half)
            up = 1.0 + th
            w = half * up
            slope = up + w * (1.0 - th)
            weights = jnp.where(visible, w * scale_row, 0.0).astype(jnp.bfloat16)
            gs = jnp.where(visible, gw * slope * scale_row, 0.0).astype(jnp.bfloat16)
            gv = gv + jnp.dot(weights, grads, preferred_element_type=jnp.float32)
            gk = gk + jnp.dot(gs, queries, preferred_element_type=jnp.float32)
            gq_s[:, pl.ds(query_row, tile)] += jnp.dot(keys_t, gs, preferred_element_type=jnp.float32)
            return gk, gv

        zero = jnp.zeros((tile, DH), jnp.float32)
        gk, gv = lax.fori_loop(key_block, stop, step, (zero, zero))
        gk_s[pl.ds(key_row, tile), :] = gk
        gv_s[pl.ds(key_row, tile), :] = gv

    @pl.loop(0, slots)
    def _(slot):
        row = pl.multiple_of(perm_ref[0, slot] * BLK, BLK)
        pre = x_ref[slot][:, : 3 * DH].astype(jnp.float32)
        sigma = jax.nn.sigmoid(pre)
        slope = sigma * (1.0 + pre * (1.0 - sigma))
        gq = gq_s[:, pl.ds(row, BLK)].T * 0.0625
        gk = gk_s[pl.ds(row, BLK), :]
        gv = gv_s[pl.ds(row, BLK), :]
        out_ref[slot, :DH, :] = (gq * slope[:, :DH]).T.astype(jnp.bfloat16)
        out_ref[slot, DH : 2 * DH, :] = (gk * slope[:, DH : 2 * DH]).T.astype(jnp.bfloat16)
        out_ref[slot, 2 * DH :, :] = (gv * slope[:, 2 * DH :]).T.astype(jnp.bfloat16)


def attention(packed, lengths, perm, tile=256):
    slots = packed.shape[0]
    whole = slots * BLK
    vmem = pl.BlockSpec(memory_space=pltpu.VMEM)
    smem = pl.BlockSpec(memory_space=pltpu.SMEM)
    bf, f32 = jnp.bfloat16, jnp.float32
    return pl.pallas_call(
        functools.partial(attention_kernel, tile),
        out_shape=jax.ShapeDtypeStruct((slots, 3 * DH, BLK), bf),
        in_specs=[smem, smem, vmem],
        out_specs=vmem,
        scratch_shapes=[
            pltpu.VMEM((whole, DH), bf),
            pltpu.VMEM((whole, DH), bf),
            pltpu.VMEM((whole, DH), bf),
            pltpu.VMEM((whole, DH), bf),
            pltpu.VMEM((DH, whole), bf),
            pltpu.VMEM((DH, whole), f32),
            pltpu.VMEM((whole, DH), f32),
            pltpu.VMEM((whole, DH), f32),
            pltpu.VMEM((whole // tile, tile), jnp.int32),
            pltpu.VMEM((whole // tile, tile), f32),
        ],
        compiler_params=pltpu.CompilerParams(vmem_limit_bytes=32 << 20),
    )(lengths, perm, packed)


class Links:
    def __init__(self, send_sem, recv_sem):
        self.send_sem, self.recv_sem = send_sem, recv_sem
        self.copies = []

    def start(self, src, dst, device):
        k = len(self.copies)
        copy = pltpu.make_async_remote_copy(
            src_ref=src,
            dst_ref=dst,
            send_sem=self.send_sem.at[k],
            recv_sem=self.recv_sem.at[k],
            device_id=device,
            device_id_type=MESH,
        )
        copy.start()
        self.copies.append(copy)
        return copy

    def wait_sends(self):
        for copy in self.copies:
            copy.wait_send()


def far_first(n):
    order = []
    for near in range(n // 2, 0, -1):
        order += sorted({near, n - near})
    return order


def all_to_all_start(links, axis, me, n, src_ref, dst_ref):
    copies = []
    for step in far_first(n):
        peer = lax.rem(me + step, n)
        copies.append(links.start(src_ref.at[peer], dst_ref.at[me], {axis: peer}))
    return copies


def ring_gather(links, me, n, own_ref, all_ref):
    rows = own_ref.shape[0] // 2
    right, left = {"ctx": lax.rem(me + 1, n)}, {"ctx": lax.rem(me + n - 1, n)}
    part = [pl.ds(0, rows), pl.ds(rows, rows)]
    far = n // 2
    ahead, back = {}, {}
    for half in range(2):
        ahead[1, half] = links.start(own_ref.at[part[half]], all_ref.at[me, part[half]], right)
        back[1, half] = links.start(own_ref.at[part[half]], all_ref.at[me, part[half]], left)
    for step in range(1, far):
        below, above = lax.rem(me + n - step, n), lax.rem(me + step, n)
        yield
        for half in range(2):
            ahead[step, half].wait_recv()
            if step < far - 1 or half == 0:
                ref = all_ref.at[below, part[half]]
                ahead[step + 1, half] = links.start(ref, ref, right)
            back[step, half].wait_recv()
            if step < far - 1 or half == 1:
                ref = all_ref.at[above, part[half]]
                back[step + 1, half] = links.start(ref, ref, left)
    yield
    ahead[far, 0].wait_recv()
    back[far, 1].wait_recv()


def plane_gather(links, own_ref, all_ref, side=4):
    dp = lax.axis_index("dp")
    core = lax.rem(dp, 2)
    chip = lax.div(dp, 2)
    x, y = lax.rem(chip, side), lax.div(chip, side)
    a = x * (1 - core) + y * core
    b = y * (1 - core) + x * core
    partner = {"dp": dp + 1 - 2 * core}
    depth = own_ref.shape[0] // 2
    part = [pl.ds(0, depth), pl.ds(depth, depth)]

    def index(i, j):
        p, q = lax.rem(a + i + side, side), lax.rem(b + j + side, side)
        px = p * (1 - core) + q * core
        py = q * (1 - core) + p * core
        return (py * side + px) * 2 + core

    def device(i, j):
        return {"dp": index(i, j)}

    across = []

    def hand_over(i, j, src=None):
        ref = all_ref.at[index(i, j)]
        across.append(links.start(ref if src is None else src, ref, partner))

    def spread(i, src=None):
        ref = all_ref.at[index(i, 0)]
        src = ref if src is None else src
        up = links.start(src, ref, device(0, 1))
        down = links.start(src, ref, device(0, -1))
        hand_over(i, 0, src)
        return up, down

    def pass_on(i, pair):
        up, down = pair
        up.wait_recv()
        ref = all_ref.at[index(i, -1), part[1]]
        far_up = links.start(ref, ref, device(0, 1))
        hand_over(i, -1)
        down.wait_recv()
        ref = all_ref.at[index(i, 1), part[0]]
        far_down = links.start(ref, ref, device(0, -1))
        hand_over(i, 1)
        return far_up, far_down

    def finish(i, pair):
        pair[0].wait_recv()
        pair[1].wait_recv()
        hand_over(i, 2)

    own_slot = all_ref.at[index(0, 0)]
    up = links.start(own_ref, own_slot, device(1, 0))
    down = links.start(own_ref, own_slot, device(-1, 0))
    first = spread(0, own_ref)
    yield
    up.wait_recv()
    ref = all_ref.at[index(-1, 0), part[1]]
    far_up = links.start(ref, ref, device(1, 0))
    second = spread(-1)
    yield
    down.wait_recv()
    ref = all_ref.at[index(1, 0), part[0]]
    far_down = links.start(ref, ref, device(-1, 0))
    third = spread(1)
    yield
    first = pass_on(0, first)
    yield
    far_up.wait_recv()
    far_down.wait_recv()
    fourth = spread(2)
    yield
    second = pass_on(-1, second)
    yield
    third = pass_on(1, third)
    yield
    finish(0, first)
    fourth = pass_on(2, fourth)
    yield
    finish(-1, second)
    finish(1, third)
    yield
    finish(2, fourth)
    yield
    for copy in across:
        copy.wait_recv()


PLANE_COPIES = 2 + 2 + 4 * 4 + 16


def greet(axis_peers):
    barrier = pltpu.get_barrier_semaphore()
    for device in axis_peers:
        pl.semaphore_signal(barrier, inc=1, device_id=device, device_id_type=MESH)
    return barrier, len(axis_peers)


def gather_kernel(n, packed_ref, tokens_ref, w_ref, recv_ref, tokens_all_ref, w_all_ref, w_rows, send_sem, recv_sem, local_sem):
    me = lax.axis_index("ctx")
    dp = lax.axis_index("dp")
    core = lax.rem(dp, 2)
    chip = lax.div(dp, 2)
    x, y = lax.rem(chip, 4), lax.div(chip, 4)
    peers = [{"ctx": lax.rem(me + step, n)} for step in range(1, n)]
    peers += [{"dp": dp + 1 - 2 * core}]
    peers += [{"dp": (y * 4 + lax.rem(x + step, 4)) * 2 + core} for step in (1, 3)]
    peers += [{"dp": (lax.rem(y + step, 4) * 4 + x) * 2 + core} for step in (1, 3)]
    barrier, count = greet(peers)
    links = Links(send_sem, recv_sem)
    own_w = pltpu.make_async_copy(w_ref, w_rows.at[me], local_sem.at[0])
    own_w.start()
    own_block = pltpu.make_async_copy(packed_ref.at[me], recv_ref.at[me], local_sem.at[1])
    own_block.start()
    own_tokens = pltpu.make_async_copy(tokens_ref, tokens_all_ref.at[me], local_sem.at[2])
    own_tokens.start()
    pl.semaphore_wait(barrier, count)
    rows_in = []
    for step in far_first(n):
        rows_in.append(links.start(w_ref, w_rows.at[me], {"ctx": lax.rem(me + step, n)}))
    ring = ring_gather(links, me, n, tokens_ref, tokens_all_ref)
    next(ring)
    blocks_in = all_to_all_start(links, "ctx", me, n, packed_ref, recv_ref)
    own_w.wait()
    for copy in rows_in:
        copy.wait_recv()
    own_rows = pltpu.make_async_copy(w_rows, w_all_ref.at[dp], local_sem.at[0])
    own_rows.start()
    plane = plane_gather(links, w_rows, w_all_ref)
    going = [plane, ring]
    while going:
        for chain in list(going):
            try:
                next(chain)
            except StopIteration:
                going.remove(chain)
    for copy in blocks_in:
        copy.wait_recv()
    links.wait_sends()
    own_rows.wait()
    own_block.wait()
    own_tokens.wait()


def gather(packed, tokens, w, planes):
    n = packed.shape[0]
    copies = (n - 1) * 2 + 2 * (n - 1) + PLANE_COPIES
    return pl.pallas_call(
        functools.partial(gather_kernel, n),
        out_shape=(
            jax.ShapeDtypeStruct(packed.shape, packed.dtype),
            jax.ShapeDtypeStruct((n,) + tokens.shape, tokens.dtype),
            jax.ShapeDtypeStruct((planes, n) + w.shape, w.dtype),
        ),
        in_specs=[VMEM, VMEM, VMEM],
        out_specs=(VMEM, ANY, ANY),
        scratch_shapes=[
            pltpu.VMEM((n,) + w.shape, w.dtype),
            pltpu.SemaphoreType.DMA((copies,)),
            pltpu.SemaphoreType.DMA((copies,)),
            pltpu.SemaphoreType.DMA((3,)),
        ],
        compiler_params=pltpu.CompilerParams(
            collective_id=1, has_side_effects=True, vmem_limit_bytes=16 << 20
        ),
    )(packed, tokens, w)


def return_kernel(n, planes, grad_ref, part_ref, back_ref, parts_ref, send_sem, recv_sem, local_sem):
    me = lax.axis_index("ctx")
    dp = lax.axis_index("dp")
    peers = [{"ctx": lax.rem(me + step, n)} for step in range(1, n)]
    peers += [{"dp": lax.rem(dp + step, planes)} for step in range(1, planes)]
    barrier, count = greet(peers)
    own_block = pltpu.make_async_copy(grad_ref.at[me], back_ref.at[me], local_sem.at[0])
    own_block.start()
    own_part = pltpu.make_async_copy(part_ref.at[dp], parts_ref.at[dp], local_sem.at[1])
    own_part.start()
    pl.semaphore_wait(barrier, count)
    links = Links(send_sem, recv_sem)
    copies = all_to_all_start(links, "ctx", me, n, grad_ref, back_ref)
    copies += all_to_all_start(links, "dp", dp, planes, part_ref, parts_ref)
    own_block.wait()
    own_part.wait()
    for copy in copies:
        copy.wait()


def send_back(grad_t, parts):
    n, planes = grad_t.shape[0], parts.shape[0]
    copies = n + planes - 2
    return pl.pallas_call(
        functools.partial(return_kernel, n, planes),
        out_shape=(
            jax.ShapeDtypeStruct(grad_t.shape, grad_t.dtype),
            jax.ShapeDtypeStruct(parts.shape, parts.dtype),
        ),
        in_specs=[VMEM, VMEM],
        out_specs=(VMEM, VMEM),
        scratch_shapes=[
            pltpu.SemaphoreType.DMA((copies,)),
            pltpu.SemaphoreType.DMA((copies,)),
            pltpu.SemaphoreType.DMA((2,)),
        ],
        compiler_params=pltpu.CompilerParams(
            collective_id=2, has_side_effects=True, vmem_limit_bytes=16 << 20
        ),
    )(grad_t, parts)


def input_grad_kernel(back_ref, w_ref, out_ref, total):
    step = pl.program_id(0)
    planes, group, rows, columns = w_ref.shape
    block = w_ref[:, 0].reshape(planes * rows, columns)
    term = jnp.dot(block, back_ref[0], preferred_element_type=jnp.float32)
    term = term.astype(jnp.bfloat16).astype(jnp.float32)

    @pl.when(step == 0)
    def _():
        total[...] = term

    @pl.when(step > 0)
    def _():
        total[...] += term

    @pl.when(step == pl.num_programs(0) - 1)
    def _():
        out_ref[...] = total[...].T.astype(out_ref.dtype)


def input_grad(back_t, w_all):
    n, columns, tokens = back_t.shape
    planes, _, rows, _ = w_all.shape
    width = planes * rows
    return pl.pallas_call(
        input_grad_kernel,
        grid=(n,),
        out_shape=jax.ShapeDtypeStruct((tokens, width), jnp.bfloat16),
        in_specs=[
            pl.BlockSpec((1, columns, tokens), lambda i: (i, 0, 0)),
            pl.BlockSpec((planes, 1, rows, columns), lambda i: (0, i, 0, 0)),
        ],
        out_specs=pl.BlockSpec((tokens, width), lambda i: (0, 0)),
        scratch_shapes=[pltpu.VMEM((width, tokens), jnp.float32)],
        compiler_params=pltpu.CompilerParams(dimension_semantics=("arbitrary",)),
    )(back_t, w_all)


def body(layer_input, projected, grad_output, w_qkv, lengths, block_perm):
    tokens_dev = layer_input.shape[1]
    width = layer_input.shape[2]
    ctx_count = lax.axis_size("ctx")
    data_count = lax.axis_size("dp")
    columns = 3 * DH
    packed = jnp.concatenate(
        [
            projected[0].reshape(tokens_dev, ctx_count, columns),
            grad_output[0].reshape(tokens_dev, ctx_count, DH),
        ],
        axis=2,
    ).transpose(1, 0, 2)
    blocks, tokens_all, w_all = gather(packed, layer_input[0], w_qkv, data_count)
    grad_t = attention(blocks, lengths, block_perm)
    weight_local = lax.dot_general(
        tokens_all.reshape(ctx_count * tokens_dev, width),
        grad_t.transpose(1, 0, 2).reshape(columns, ctx_count * tokens_dev),
        (((0,), (1,)), ((), ())),
        preferred_element_type=jnp.float32,
    )
    parts = weight_local.reshape(data_count, width // data_count, columns)
    back_t, parts = send_back(grad_t, parts)
    grad_weight = jnp.sum(parts, axis=0) * (1.0 / data_count)
    return (input_grad(back_t, w_all)[None], grad_weight)


def solution(mesh):
    return jax.shard_map(
        body,
        mesh=mesh,
        in_specs=(
            P("dp", "ctx", None),
            P("dp", "ctx", None),
            P("dp", "ctx", None),
            P("dp", "ctx"),
            P("dp", None),
            P("dp", None),
        ),
        out_specs=(P("dp", "ctx", None), P("dp", "ctx")),
        check_vma=False,
    )
```

```python
import functools

import jax
import jax.numpy as jnp
from jax import lax
from jax.experimental import pallas as pl
from jax.experimental.pallas import tpu as pltpu
from jax.sharding import PartitionSpec as P

DH = 64
BLK = 128
MESH = pl.DeviceIdType.MESH
VMEM = pl.BlockSpec(memory_space=pltpu.VMEM)
ANY = pl.BlockSpec(memory_space=pl.ANY)


def attention_kernel(tile, lengths_ref, perm_ref, x_ref, out_ref, q_s, k_s, v_s, g_s, kt_s, gq_s, gk_s, gv_s, start_s, scale_s):
    slots = x_ref.shape[0]
    whole = slots * BLK
    users = lengths_ref.shape[1]
    count = whole // tile

    pos = lax.broadcasted_iota(jnp.int32, (count, tile), 0) * tile + lax.broadcasted_iota(jnp.int32, (count, tile), 1)
    first = jnp.zeros((count, tile), jnp.int32)
    length = jnp.ones((count, tile), jnp.int32)
    end = jnp.int32(0)
    for user in range(users):
        begin = end
        end = begin + lengths_ref[0, user]
        inside = pos >= begin
        first = jnp.where(inside, begin, first)
        length = jnp.where(inside, lengths_ref[0, user], length)
    start_s[...] = first
    scale_s[...] = lax.rsqrt(length.astype(jnp.float32))

    @pl.loop(0, slots)
    def _(slot):
        row = pl.multiple_of(perm_ref[0, slot] * BLK, BLK)
        block = x_ref[slot]
        pre = block[:, : 3 * DH].astype(jnp.float32)
        active = (pre * jax.nn.sigmoid(pre)).astype(jnp.bfloat16)
        q_s[pl.ds(row, BLK), :] = active[:, :DH] * jnp.bfloat16(0.0625)
        key = active[:, DH : 2 * DH]
        k_s[pl.ds(row, BLK), :] = key
        kt_s[:, pl.ds(row, BLK)] = key.T
        v_s[pl.ds(row, BLK), :] = active[:, 2 * DH :]
        g_s[pl.ds(row, BLK), :] = block[:, 3 * DH :]

    gq_s[...] = jnp.zeros_like(gq_s)
    contract = (((1,), (1,)), ((), ()))

    @pl.loop(0, count)
    def _(key_block):
        key_row = pl.multiple_of(key_block * tile, tile)
        last_key = key_row + tile - 1
        limit = jnp.int32(0)
        total = jnp.int32(0)
        for user in range(users):
            begin = total
            total = begin + lengths_ref[0, user]
            limit = jnp.where(last_key >= begin, total, limit)
        stop = (limit + tile - 1) // tile
        keys = k_s[pl.ds(key_row, tile), :]
        values = v_s[pl.ds(key_row, tile), :]
        keys_t = kt_s[:, pl.ds(key_row, tile)]
        key_pos = key_row + lax.broadcasted_iota(jnp.int32, (tile, 1), 0)

        def step(query_block, carry):
            gk, gv = carry
            query_row = pl.multiple_of(query_block * tile, tile)
            queries = q_s[pl.ds(query_row, tile), :]
            grads = g_s[pl.ds(query_row, tile), :]
            half = lax.dot_general(keys, queries, contract, preferred_element_type=jnp.float32)
            gw = lax.dot_general(values, grads, contract, preferred_element_type=jnp.float32)
            first_row = start_s[pl.ds(query_block, 1), :]
            scale_row = scale_s[pl.ds(query_block, 1), :]
            query_pos = query_row + lax.broadcasted_iota(jnp.int32, (1, tile), 1)
            visible = (key_pos >= first_row) & (key_pos <= query_pos)
            th = jnp.tanh(half)
            up = 1.0 + th
            w = half * up
            slope = up + w * (1.0 - th)
            weights = jnp.where(visible, w * scale_row, 0.0).astype(jnp.bfloat16)
            gs = jnp.where(visible, gw * slope * scale_row, 0.0).astype(jnp.bfloat16)
            gv = gv + jnp.dot(weights, grads, preferred_element_type=jnp.float32)
            gk = gk + jnp.dot(gs, queries, preferred_element_type=jnp.float32)
            gq_s[:, pl.ds(query_row, tile)] += jnp.dot(keys_t, gs, preferred_element_type=jnp.float32)
            return gk, gv

        zero = jnp.zeros((tile, DH), jnp.float32)
        gk, gv = lax.fori_loop(key_block, stop, step, (zero, zero))
        gk_s[pl.ds(key_row, tile), :] = gk
        gv_s[pl.ds(key_row, tile), :] = gv

    @pl.loop(0, slots)
    def _(slot):
        row = pl.multiple_of(perm_ref[0, slot] * BLK, BLK)
        pre = x_ref[slot][:, : 3 * DH].astype(jnp.float32)
        sigma = jax.nn.sigmoid(pre)
        slope = sigma * (1.0 + pre * (1.0 - sigma))
        gq = gq_s[:, pl.ds(row, BLK)].T * 0.0625
        gk = gk_s[pl.ds(row, BLK), :]
        gv = gv_s[pl.ds(row, BLK), :]
        out_ref[slot, :DH, :] = (gq * slope[:, :DH]).T.astype(jnp.bfloat16)
        out_ref[slot, DH : 2 * DH, :] = (gk * slope[:, DH : 2 * DH]).T.astype(jnp.bfloat16)
        out_ref[slot, 2 * DH :, :] = (gv * slope[:, 2 * DH :]).T.astype(jnp.bfloat16)


def attention(packed, lengths, perm, tile=256):
    slots = packed.shape[0]
    whole = slots * BLK
    vmem = pl.BlockSpec(memory_space=pltpu.VMEM)
    smem = pl.BlockSpec(memory_space=pltpu.SMEM)
    bf, f32 = jnp.bfloat16, jnp.float32
    return pl.pallas_call(
        functools.partial(attention_kernel, tile),
        out_shape=jax.ShapeDtypeStruct((slots, 3 * DH, BLK), bf),
        in_specs=[smem, smem, vmem],
        out_specs=vmem,
        scratch_shapes=[
            pltpu.VMEM((whole, DH), bf),
            pltpu.VMEM((whole, DH), bf),
            pltpu.VMEM((whole, DH), bf),
            pltpu.VMEM((whole, DH), bf),
            pltpu.VMEM((DH, whole), bf),
            pltpu.VMEM((DH, whole), f32),
            pltpu.VMEM((whole, DH), f32),
            pltpu.VMEM((whole, DH), f32),
            pltpu.VMEM((whole // tile, tile), jnp.int32),
            pltpu.VMEM((whole // tile, tile), f32),
        ],
        compiler_params=pltpu.CompilerParams(vmem_limit_bytes=32 << 20),
    )(lengths, perm, packed)


class Links:
    def __init__(self, send_sem, recv_sem):
        self.send_sem, self.recv_sem = send_sem, recv_sem
        self.copies = []

    def start(self, src, dst, device):
        k = len(self.copies)
        copy = pltpu.make_async_remote_copy(
            src_ref=src,
            dst_ref=dst,
            send_sem=self.send_sem.at[k],
            recv_sem=self.recv_sem.at[k],
            device_id=device,
            device_id_type=MESH,
        )
        copy.start()
        self.copies.append(copy)
        return copy

    def wait_sends(self):
        for copy in self.copies:
            copy.wait_send()


def far_first(n):
    order = []
    for near in range(n // 2, 0, -1):
        order += sorted({near, n - near})
    return order


def all_to_all_start(links, axis, me, n, src_ref, dst_ref):
    copies = []
    for step in far_first(n):
        peer = lax.rem(me + step, n)
        copies.append(links.start(src_ref.at[peer], dst_ref.at[me], {axis: peer}))
    return copies


def plane_gather(links, own_ref, all_ref, side=4):
    dp = lax.axis_index("dp")
    core = lax.rem(dp, 2)
    chip = lax.div(dp, 2)
    x, y = lax.rem(chip, side), lax.div(chip, side)
    a = x * (1 - core) + y * core
    b = y * (1 - core) + x * core
    partner = {"dp": dp + 1 - 2 * core}
    depth = own_ref.shape[0] // 2
    part = [pl.ds(0, depth), pl.ds(depth, depth)]

    def index(i, j):
        p, q = lax.rem(a + i + side, side), lax.rem(b + j + side, side)
        px = p * (1 - core) + q * core
        py = q * (1 - core) + p * core
        return (py * side + px) * 2 + core

    def device(i, j):
        return {"dp": index(i, j)}

    across = []

    def hand_over(i, j, src=None):
        ref = all_ref.at[index(i, j)]
        across.append(links.start(ref if src is None else src, ref, partner))

    def spread(i, src=None):
        ref = all_ref.at[index(i, 0)]
        src = ref if src is None else src
        up = links.start(src, ref, device(0, 1))
        down = links.start(src, ref, device(0, -1))
        hand_over(i, 0, src)
        return up, down

    def pass_on(i, pair):
        up, down = pair
        up.wait_recv()
        ref = all_ref.at[index(i, -1), part[1]]
        far_up = links.start(ref, ref, device(0, 1))
        hand_over(i, -1)
        down.wait_recv()
        ref = all_ref.at[index(i, 1), part[0]]
        far_down = links.start(ref, ref, device(0, -1))
        hand_over(i, 1)
        return far_up, far_down

    def finish(i, pair):
        pair[0].wait_recv()
        pair[1].wait_recv()
        hand_over(i, 2)

    own_slot = all_ref.at[index(0, 0)]
    up = links.start(own_ref, own_slot, device(1, 0))
    down = links.start(own_ref, own_slot, device(-1, 0))
    first = spread(0, own_ref)
    yield
    up.wait_recv()
    ref = all_ref.at[index(-1, 0), part[1]]
    far_up = links.start(ref, ref, device(1, 0))
    second = spread(-1)
    yield
    down.wait_recv()
    ref = all_ref.at[index(1, 0), part[0]]
    far_down = links.start(ref, ref, device(-1, 0))
    third = spread(1)
    yield
    first = pass_on(0, first)
    yield
    far_up.wait_recv()
    far_down.wait_recv()
    fourth = spread(2)
    yield
    second = pass_on(-1, second)
    yield
    third = pass_on(1, third)
    yield
    finish(0, first)
    fourth = pass_on(2, fourth)
    yield
    finish(-1, second)
    finish(1, third)
    yield
    finish(2, fourth)
    yield
    for copy in across:
        copy.wait_recv()


PLANE_COPIES = 2 + 2 + 4 * 4 + 16


def greet(axis_peers):
    barrier = pltpu.get_barrier_semaphore()
    for device in axis_peers:
        pl.semaphore_signal(barrier, inc=1, device_id=device, device_id_type=MESH)
    return barrier, len(axis_peers)


def ring_peers(me, n):
    return [{"ctx": lax.rem(me + step, n)} for step in range(1, n)]


def plane_peers(dp, planes):
    return [{"dp": lax.rem(dp + step, planes)} for step in range(1, planes)]


def gather_kernel(n, packed_ref, tokens_ref, w_ref, recv_ref, tokens_all_ref, w_rows_ref, send_sem, recv_sem, local_sem):
    me = lax.axis_index("ctx")
    dp = lax.axis_index("dp")
    core = lax.rem(dp, 2)
    chip = lax.div(dp, 2)
    x, y = lax.rem(chip, 4), lax.div(chip, 4)
    peers = ring_peers(me, n)
    peers += [{"dp": dp + 1 - 2 * core}]
    peers += [{"dp": (y * 4 + lax.rem(x + step, 4)) * 2 + core} for step in (1, 3)]
    peers += [{"dp": (lax.rem(y + step, 4) * 4 + x) * 2 + core} for step in (1, 3)]
    barrier, count = greet(peers)
    links = Links(send_sem, recv_sem)
    own = [
        pltpu.make_async_copy(packed_ref.at[me], recv_ref.at[me], local_sem.at[0]),
        pltpu.make_async_copy(tokens_ref, tokens_all_ref.at[dp], local_sem.at[1]),
        pltpu.make_async_copy(w_ref, w_rows_ref.at[me], local_sem.at[2]),
    ]
    for copy in own:
        copy.start()
    pl.semaphore_wait(barrier, count)
    plane = plane_gather(links, tokens_ref, tokens_all_ref)
    next(plane)
    copies = all_to_all_start(links, "ctx", me, n, packed_ref, recv_ref)
    for step in far_first(n):
        copies.append(links.start(w_ref, w_rows_ref.at[me], {"ctx": lax.rem(me + step, n)}))
    for _ in plane:
        pass
    for copy in copies:
        copy.wait_recv()
    links.wait_sends()
    for copy in own:
        copy.wait()


def gather(packed, tokens, w, planes):
    n = packed.shape[0]
    copies = (n - 1) * 2 + PLANE_COPIES
    return pl.pallas_call(
        functools.partial(gather_kernel, n),
        out_shape=(
            jax.ShapeDtypeStruct(packed.shape, packed.dtype),
            jax.ShapeDtypeStruct((planes,) + tokens.shape, tokens.dtype),
            jax.ShapeDtypeStruct((n,) + w.shape, w.dtype),
        ),
        in_specs=[VMEM, VMEM, VMEM],
        out_specs=(VMEM, ANY, VMEM),
        scratch_shapes=[
            pltpu.SemaphoreType.DMA((copies,)),
            pltpu.SemaphoreType.DMA((copies,)),
            pltpu.SemaphoreType.DMA((3,)),
        ],
        compiler_params=pltpu.CompilerParams(
            collective_id=1, has_side_effects=True, vmem_limit_bytes=16 << 20
        ),
    )(packed, tokens, w)


def return_kernel(n, planes, grad_ref, w_rows_ref, back_ref, cols_ref, w_all_ref, send_sem, recv_sem, local_sem):
    me = lax.axis_index("ctx")
    dp = lax.axis_index("dp")
    half = cols_ref.shape[1]
    barrier, count = greet(ring_peers(me, n) + plane_peers(dp, planes))
    own_block = pltpu.make_async_copy(grad_ref.at[me], back_ref.at[me], local_sem.at[0])
    own_block.start()
    own_rows = pltpu.make_async_copy(w_rows_ref, w_all_ref.at[dp], local_sem.at[1])
    own_rows.start()
    pl.semaphore_wait(barrier, count)
    links = Links(send_sem, recv_sem)
    copies = all_to_all_start(links, "ctx", me, n, grad_ref, back_ref)
    for _ in plane_gather(links, w_rows_ref, w_all_ref):
        pass
    own_block.wait()
    for copy in copies:
        copy.wait_recv()

    def chunk(owner):
        start = pl.multiple_of(lax.rem(owner, 2) * half, half)
        return back_ref.at[lax.div(owner, 2), pl.ds(start, half)]

    copies = []
    for step in far_first(planes):
        owner = lax.rem(dp + step, planes)
        copies.append(links.start(chunk(owner), cols_ref.at[dp], {"dp": owner}))
    own_cols = pltpu.make_async_copy(chunk(dp), cols_ref.at[dp], local_sem.at[2])
    own_cols.start()
    for copy in copies:
        copy.wait_recv()
    links.wait_sends()
    own_rows.wait()
    own_cols.wait()


def send_back(grad_t, w_rows, planes):
    n, columns, tokens = grad_t.shape
    copies = n - 1 + planes - 1 + PLANE_COPIES
    return pl.pallas_call(
        functools.partial(return_kernel, n, planes),
        out_shape=(
            jax.ShapeDtypeStruct(grad_t.shape, grad_t.dtype),
            jax.ShapeDtypeStruct((planes, n * columns // planes, tokens), grad_t.dtype),
            jax.ShapeDtypeStruct((planes,) + w_rows.shape, w_rows.dtype),
        ),
        in_specs=[VMEM, VMEM],
        out_specs=(VMEM, VMEM, ANY),
        scratch_shapes=[
            pltpu.SemaphoreType.DMA((copies,)),
            pltpu.SemaphoreType.DMA((copies,)),
            pltpu.SemaphoreType.DMA((3,)),
        ],
        compiler_params=pltpu.CompilerParams(
            collective_id=2, has_side_effects=True, vmem_limit_bytes=16 << 20
        ),
    )(grad_t, w_rows)


def weight_grad_kernel(cols_ref, tokens_ref, out_ref, total):
    step = pl.program_id(0)
    group, tokens, width = tokens_ref.shape
    left = jnp.concatenate([cols_ref[i] for i in range(group)], axis=1)
    term = jnp.dot(left, tokens_ref[...].reshape(group * tokens, width), preferred_element_type=jnp.float32)

    @pl.when(step == 0)
    def _():
        total[...] = term

    @pl.when(step > 0)
    def _():
        total[...] += term

    @pl.when(step == pl.num_programs(0) - 1)
    def _():
        planes, rows, columns = out_ref.shape
        mean = total[...] * (1.0 / planes)
        out_ref[...] = mean.T.astype(out_ref.dtype).reshape(planes, rows, columns)


def weight_grad(cols, tokens_all):
    planes, columns, tokens = cols.shape
    width = tokens_all.shape[2]
    group = 4
    return pl.pallas_call(
        weight_grad_kernel,
        grid=(planes // group,),
        out_shape=jax.ShapeDtypeStruct((planes, width // planes, columns), jnp.bfloat16),
        in_specs=[
            pl.BlockSpec((group, columns, tokens), lambda i: (i, 0, 0)),
            pl.BlockSpec((group, tokens, width), lambda i: (i, 0, 0)),
        ],
        out_specs=pl.BlockSpec((planes, width // planes, columns), lambda i: (0, 0, 0)),
        scratch_shapes=[pltpu.VMEM((columns, width), jnp.float32)],
        compiler_params=pltpu.CompilerParams(dimension_semantics=("arbitrary",)),
    )(cols, tokens_all)


def settle_kernel(n, planes, part_ref, out_ref, rows_ref, send_sem, recv_sem, local_sem):
    me = lax.axis_index("ctx")
    dp = lax.axis_index("dp")
    pair = planes // n
    barrier, count = greet(ring_peers(me, n) + plane_peers(dp, planes))
    own_part = pltpu.make_async_copy(part_ref.at[dp], rows_ref.at[dp], local_sem.at[0])
    own_part.start()
    pl.semaphore_wait(barrier, count)
    links = Links(send_sem, recv_sem)
    for copy in all_to_all_start(links, "dp", dp, planes, part_ref, rows_ref):
        copy.wait_recv()
    own_part.wait()

    def head(owner):
        return rows_ref.at[pl.ds(owner * pair, pair)]

    copies = []
    for step in far_first(n):
        owner = lax.rem(me + step, n)
        copies.append(links.start(head(owner), out_ref.at[me], {"ctx": owner}))
    own_head = pltpu.make_async_copy(head(me), out_ref.at[me], local_sem.at[1])
    own_head.start()
    for copy in copies:
        copy.wait_recv()
    links.wait_sends()
    own_head.wait()


def settle(parts, n):
    planes, rows, columns = parts.shape
    copies = n - 1 + planes - 1
    return pl.pallas_call(
        functools.partial(settle_kernel, n, planes),
        out_shape=jax.ShapeDtypeStruct((n, planes // n, rows, columns), parts.dtype),
        in_specs=[VMEM],
        out_specs=VMEM,
        scratch_shapes=[
            pltpu.VMEM(parts.shape, parts.dtype),
            pltpu.SemaphoreType.DMA((copies,)),
            pltpu.SemaphoreType.DMA((copies,)),
            pltpu.SemaphoreType.DMA((2,)),
        ],
        compiler_params=pltpu.CompilerParams(
            collective_id=3, has_side_effects=True, vmem_limit_bytes=16 << 20
        ),
    )(parts)


def input_grad_kernel(back_ref, w_ref, out_ref, total):
    step = pl.program_id(0)
    planes, group, rows, columns = w_ref.shape
    term = jnp.zeros(total.shape, jnp.float32)
    for i in range(group):
        block = w_ref[:, i].reshape(planes * rows, columns)
        part = jnp.dot(block, back_ref[i], preferred_element_type=jnp.float32)
        term = term + part.astype(jnp.bfloat16).astype(jnp.float32)

    @pl.when(step == 0)
    def _():
        total[...] = term

    @pl.when(step > 0)
    def _():
        total[...] += term

    @pl.when(step == pl.num_programs(0) - 1)
    def _():
        out_ref[...] = total[...].T.astype(out_ref.dtype)


def input_grad(back_t, w_all):
    n, columns, tokens = back_t.shape
    planes, _, rows, _ = w_all.shape
    width = planes * rows
    group = 4
    return pl.pallas_call(
        input_grad_kernel,
        grid=(n // group,),
        out_shape=jax.ShapeDtypeStruct((tokens, width), jnp.bfloat16),
        in_specs=[
            pl.BlockSpec((group, columns, tokens), lambda i: (i, 0, 0)),
            pl.BlockSpec((planes, group, rows, columns), lambda i: (0, i, 0, 0)),
        ],
        out_specs=pl.BlockSpec((tokens, width), lambda i: (0, 0)),
        scratch_shapes=[pltpu.VMEM((width, tokens), jnp.float32)],
        compiler_params=pltpu.CompilerParams(dimension_semantics=("arbitrary",)),
    )(back_t, w_all)


def body(layer_input, projected, grad_output, w_qkv, lengths, block_perm):
    tokens_dev = layer_input.shape[1]
    width = layer_input.shape[2]
    ctx_count = lax.axis_size("ctx")
    data_count = lax.axis_size("dp")
    columns = 3 * DH
    packed = jnp.concatenate(
        [
            projected[0].reshape(tokens_dev, ctx_count, columns),
            grad_output[0].reshape(tokens_dev, ctx_count, DH),
        ],
        axis=2,
    ).transpose(1, 0, 2)
    blocks, tokens_all, w_rows = gather(packed, layer_input[0], w_qkv, data_count)
    grad_t = attention(blocks, lengths, block_perm)
    back_t, cols, w_all = send_back(grad_t, w_rows, data_count)
    parts = settle(weight_grad(cols, tokens_all), ctx_count)
    grad_weight = jnp.sum(parts.astype(jnp.float32), axis=0).transpose(1, 0, 2)
    grad_weight = grad_weight.reshape(width // data_count, columns)
    return (input_grad(back_t, w_all)[None], grad_weight)


def solution(mesh):
    return jax.shard_map(
        body,
        mesh=mesh,
        in_specs=(
            P("dp", "ctx", None),
            P("dp", "ctx", None),
            P("dp", "ctx", None),
            P("dp", "ctx"),
            P("dp", None),
            P("dp", None),
        ),
        out_specs=(P("dp", "ctx", None), P("dp", "ctx")),
        check_vma=False,
    )
```

```python
import functools

import jax
import jax.numpy as jnp
from jax import lax
from jax.experimental import pallas as pl
from jax.experimental.pallas import tpu as pltpu
from jax.sharding import PartitionSpec as P

DH = 64
BLK = 128
MESH = pl.DeviceIdType.MESH
VMEM = pl.BlockSpec(memory_space=pltpu.VMEM)


def attention_kernel(tile, lengths_ref, perm_ref, x_ref, out_ref, q_s, k_s, v_s, g_s, kt_s, gq_s, gk_s, gv_s, start_s, scale_s):
    slots = x_ref.shape[0]
    whole = slots * BLK
    users = lengths_ref.shape[1]
    count = whole // tile

    pos = lax.broadcasted_iota(jnp.int32, (count, tile), 0) * tile + lax.broadcasted_iota(jnp.int32, (count, tile), 1)
    first = jnp.zeros((count, tile), jnp.int32)
    length = jnp.ones((count, tile), jnp.int32)
    end = jnp.int32(0)
    for user in range(users):
        begin = end
        end = begin + lengths_ref[0, user]
        inside = pos >= begin
        first = jnp.where(inside, begin, first)
        length = jnp.where(inside, lengths_ref[0, user], length)
    start_s[...] = first
    scale_s[...] = lax.rsqrt(length.astype(jnp.float32))

    @pl.loop(0, slots)
    def _(slot):
        row = pl.multiple_of(perm_ref[0, slot] * BLK, BLK)
        block = x_ref[slot]
        pre = block[:, : 3 * DH].astype(jnp.float32)
        active = (pre * jax.nn.sigmoid(pre)).astype(jnp.bfloat16)
        q_s[pl.ds(row, BLK), :] = active[:, :DH] * jnp.bfloat16(0.0625)
        key = active[:, DH : 2 * DH]
        k_s[pl.ds(row, BLK), :] = key
        kt_s[:, pl.ds(row, BLK)] = key.T
        v_s[pl.ds(row, BLK), :] = active[:, 2 * DH :]
        g_s[pl.ds(row, BLK), :] = block[:, 3 * DH :]

    gq_s[...] = jnp.zeros_like(gq_s)
    contract = (((1,), (1,)), ((), ()))

    @pl.loop(0, count)
    def _(key_block):
        key_row = pl.multiple_of(key_block * tile, tile)
        last_key = key_row + tile - 1
        limit = jnp.int32(0)
        total = jnp.int32(0)
        for user in range(users):
            begin = total
            total = begin + lengths_ref[0, user]
            limit = jnp.where(last_key >= begin, total, limit)
        stop = (limit + tile - 1) // tile
        keys = k_s[pl.ds(key_row, tile), :]
        values = v_s[pl.ds(key_row, tile), :]
        keys_t = kt_s[:, pl.ds(key_row, tile)]
        key_pos = key_row + lax.broadcasted_iota(jnp.int32, (tile, 1), 0)

        def step(query_block, carry):
            gk, gv = carry
            query_row = pl.multiple_of(query_block * tile, tile)
            queries = q_s[pl.ds(query_row, tile), :]
            grads = g_s[pl.ds(query_row, tile), :]
            half = lax.dot_general(keys, queries, contract, preferred_element_type=jnp.float32)
            gw = lax.dot_general(values, grads, contract, preferred_element_type=jnp.float32)
            first_row = start_s[pl.ds(query_block, 1), :]
            scale_row = scale_s[pl.ds(query_block, 1), :]
            query_pos = query_row + lax.broadcasted_iota(jnp.int32, (1, tile), 1)
            visible = (key_pos >= first_row) & (key_pos <= query_pos)
            th = jnp.tanh(half)
            up = 1.0 + th
            w = half * up
            slope = up + w * (1.0 - th)
            weights = jnp.where(visible, w * scale_row, 0.0).astype(jnp.bfloat16)
            gs = jnp.where(visible, gw * slope * scale_row, 0.0).astype(jnp.bfloat16)
            gv = gv + jnp.dot(weights, grads, preferred_element_type=jnp.float32)
            gk = gk + jnp.dot(gs, queries, preferred_element_type=jnp.float32)
            gq_s[:, pl.ds(query_row, tile)] += jnp.dot(keys_t, gs, preferred_element_type=jnp.float32)
            return gk, gv

        zero = jnp.zeros((tile, DH), jnp.float32)
        gk, gv = lax.fori_loop(key_block, stop, step, (zero, zero))
        gk_s[pl.ds(key_row, tile), :] = gk
        gv_s[pl.ds(key_row, tile), :] = gv

    @pl.loop(0, slots)
    def _(slot):
        row = pl.multiple_of(perm_ref[0, slot] * BLK, BLK)
        pre = x_ref[slot][:, : 3 * DH].astype(jnp.float32)
        sigma = jax.nn.sigmoid(pre)
        slope = sigma * (1.0 + pre * (1.0 - sigma))
        gq = gq_s[:, pl.ds(row, BLK)].T * 0.0625
        gk = gk_s[pl.ds(row, BLK), :]
        gv = gv_s[pl.ds(row, BLK), :]
        out_ref[slot, :DH, :] = (gq * slope[:, :DH]).T.astype(jnp.bfloat16)
        out_ref[slot, DH : 2 * DH, :] = (gk * slope[:, DH : 2 * DH]).T.astype(jnp.bfloat16)
        out_ref[slot, 2 * DH :, :] = (gv * slope[:, 2 * DH :]).T.astype(jnp.bfloat16)


def attention(packed, lengths, perm, tile=256):
    slots = packed.shape[0]
    whole = slots * BLK
    vmem = pl.BlockSpec(memory_space=pltpu.VMEM)
    smem = pl.BlockSpec(memory_space=pltpu.SMEM)
    bf, f32 = jnp.bfloat16, jnp.float32
    return pl.pallas_call(
        functools.partial(attention_kernel, tile),
        out_shape=jax.ShapeDtypeStruct((slots, 3 * DH, BLK), bf),
        in_specs=[smem, smem, vmem],
        out_specs=vmem,
        scratch_shapes=[
            pltpu.VMEM((whole, DH), bf),
            pltpu.VMEM((whole, DH), bf),
            pltpu.VMEM((whole, DH), bf),
            pltpu.VMEM((whole, DH), bf),
            pltpu.VMEM((DH, whole), bf),
            pltpu.VMEM((DH, whole), f32),
            pltpu.VMEM((whole, DH), f32),
            pltpu.VMEM((whole, DH), f32),
            pltpu.VMEM((whole // tile, tile), jnp.int32),
            pltpu.VMEM((whole // tile, tile), f32),
        ],
        compiler_params=pltpu.CompilerParams(vmem_limit_bytes=24 << 20),
    )(lengths, perm, packed)


class Links:
    def __init__(self, send_sem, recv_sem):
        self.send_sem, self.recv_sem = send_sem, recv_sem
        self.copies = []

    def start(self, src, dst, device):
        k = len(self.copies)
        copy = pltpu.make_async_remote_copy(
            src_ref=src,
            dst_ref=dst,
            send_sem=self.send_sem.at[k],
            recv_sem=self.recv_sem.at[k],
            device_id=device,
            device_id_type=MESH,
        )
        copy.start()
        self.copies.append(copy)
        return copy

    def wait_sends(self):
        for copy in self.copies:
            copy.wait_send()


def far_first(n):
    order = []
    for near in range(n // 2, 0, -1):
        order += sorted({near, n - near})
    return order


def all_to_all_start(links, axis, me, n, src_ref, dst_ref):
    copies = []
    for step in far_first(n):
        peer = lax.rem(me + step, n)
        copies.append(links.start(src_ref.at[peer], dst_ref.at[me], {axis: peer}))
    return copies


def plane_gather(links, own_ref, all_ref, side=4):
    dp = lax.axis_index("dp")
    core = lax.rem(dp, 2)
    chip = lax.div(dp, 2)
    x, y = lax.rem(chip, side), lax.div(chip, side)
    a = x * (1 - core) + y * core
    b = y * (1 - core) + x * core
    partner = {"dp": dp + 1 - 2 * core}
    depth = own_ref.shape[0] // 2
    part = [pl.ds(0, depth), pl.ds(depth, depth)]

    def index(i, j):
        p, q = lax.rem(a + i + side, side), lax.rem(b + j + side, side)
        px = p * (1 - core) + q * core
        py = q * (1 - core) + p * core
        return (py * side + px) * 2 + core

    def device(i, j):
        return {"dp": index(i, j)}

    across = []

    def hand_over(i, j, src=None):
        ref = all_ref.at[index(i, j)]
        across.append(links.start(ref if src is None else src, ref, partner))

    def spread(i, src=None):
        ref = all_ref.at[index(i, 0)]
        src = ref if src is None else src
        up = links.start(src, ref, device(0, 1))
        down = links.start(src, ref, device(0, -1))
        hand_over(i, 0, src)
        return up, down

    def pass_on(i, pair):
        up, down = pair
        up.wait_recv()
        ref = all_ref.at[index(i, -1), part[1]]
        far_up = links.start(ref, ref, device(0, 1))
        hand_over(i, -1)
        down.wait_recv()
        ref = all_ref.at[index(i, 1), part[0]]
        far_down = links.start(ref, ref, device(0, -1))
        hand_over(i, 1)
        return far_up, far_down

    def finish(i, pair):
        pair[0].wait_recv()
        pair[1].wait_recv()
        hand_over(i, 2)

    own_slot = all_ref.at[index(0, 0)]
    up = links.start(own_ref, own_slot, device(1, 0))
    down = links.start(own_ref, own_slot, device(-1, 0))
    first = spread(0, own_ref)
    yield
    up.wait_recv()
    ref = all_ref.at[index(-1, 0), part[1]]
    far_up = links.start(ref, ref, device(1, 0))
    second = spread(-1)
    yield
    down.wait_recv()
    ref = all_ref.at[index(1, 0), part[0]]
    far_down = links.start(ref, ref, device(-1, 0))
    third = spread(1)
    yield
    first = pass_on(0, first)
    yield
    far_up.wait_recv()
    far_down.wait_recv()
    fourth = spread(2)
    yield
    second = pass_on(-1, second)
    yield
    third = pass_on(1, third)
    yield
    finish(0, first)
    fourth = pass_on(2, fourth)
    yield
    finish(-1, second)
    finish(1, third)
    yield
    finish(2, fourth)
    yield
    for copy in across:
        copy.wait_recv()


PLANE_COPIES = 2 + 2 + 4 * 4 + 16


def greet(axis_peers):
    barrier = pltpu.get_barrier_semaphore()
    for device in axis_peers:
        pl.semaphore_signal(barrier, inc=1, device_id=device, device_id_type=MESH)
    return barrier, len(axis_peers)


def ring_peers(me, n):
    return [{"ctx": lax.rem(me + step, n)} for step in range(1, n)]


def plane_peers(dp, planes):
    return [{"dp": lax.rem(dp + step, planes)} for step in range(1, planes)]


def gather_kernel(n, packed_ref, tokens_ref, w_ref, recv_ref, tokens_all_ref, w_rows_ref, send_sem, recv_sem, local_sem):
    me = lax.axis_index("ctx")
    dp = lax.axis_index("dp")
    core = lax.rem(dp, 2)
    chip = lax.div(dp, 2)
    x, y = lax.rem(chip, 4), lax.div(chip, 4)
    peers = ring_peers(me, n)
    peers += [{"dp": dp + 1 - 2 * core}]
    peers += [{"dp": (y * 4 + lax.rem(x + step, 4)) * 2 + core} for step in (1, 3)]
    peers += [{"dp": (lax.rem(y + step, 4) * 4 + x) * 2 + core} for step in (1, 3)]
    barrier, count = greet(peers)
    links = Links(send_sem, recv_sem)
    own = [
        pltpu.make_async_copy(packed_ref.at[me], recv_ref.at[me], local_sem.at[0]),
        pltpu.make_async_copy(tokens_ref, tokens_all_ref.at[dp], local_sem.at[1]),
        pltpu.make_async_copy(w_ref, w_rows_ref.at[me], local_sem.at[2]),
    ]
    for copy in own:
        copy.start()
    pl.semaphore_wait(barrier, count)
    plane = plane_gather(links, tokens_ref, tokens_all_ref)
    next(plane)
    copies = all_to_all_start(links, "ctx", me, n, packed_ref, recv_ref)
    for step in far_first(n):
        copies.append(links.start(w_ref, w_rows_ref.at[me], {"ctx": lax.rem(me + step, n)}))
    for _ in plane:
        pass
    for copy in copies:
        copy.wait_recv()
    links.wait_sends()
    for copy in own:
        copy.wait()


def gather(packed, tokens, w, planes):
    n = packed.shape[0]
    copies = (n - 1) * 2 + PLANE_COPIES
    return pl.pallas_call(
        functools.partial(gather_kernel, n),
        out_shape=(
            jax.ShapeDtypeStruct(packed.shape, packed.dtype),
            jax.ShapeDtypeStruct((planes,) + tokens.shape, tokens.dtype),
            jax.ShapeDtypeStruct((n,) + w.shape, w.dtype),
        ),
        in_specs=[VMEM, VMEM, VMEM],
        out_specs=(VMEM, VMEM, VMEM),
        scratch_shapes=[
            pltpu.SemaphoreType.DMA((copies,)),
            pltpu.SemaphoreType.DMA((copies,)),
            pltpu.SemaphoreType.DMA((3,)),
        ],
        compiler_params=pltpu.CompilerParams(
            collective_id=1, has_side_effects=True, vmem_limit_bytes=24 << 20
        ),
    )(packed, tokens, w)


def return_kernel(
    n, planes, grad_ref, w_rows_ref, tokens_ref, input_ref, weight_ref,
    back, cols, w_all, input_sum, weight_sum, parts, rows_in, send_sem, recv_sem, local_sem,
):
    me = lax.axis_index("ctx")
    dp = lax.axis_index("dp")
    half = cols.shape[1]
    pair = planes // n
    barrier, count = greet(ring_peers(me, n) + plane_peers(dp, planes))
    own_block = pltpu.make_async_copy(grad_ref.at[me], back.at[me], local_sem.at[0])
    own_block.start()
    own_rows = pltpu.make_async_copy(w_rows_ref, w_all.at[dp], local_sem.at[1])
    own_rows.start()
    input_sum[...] = jnp.zeros_like(input_sum)
    weight_sum[...] = jnp.zeros_like(weight_sum)
    pl.semaphore_wait(barrier, count)
    links = Links(send_sem, recv_sem)
    copies = all_to_all_start(links, "ctx", me, n, grad_ref, back)
    for _ in plane_gather(links, w_rows_ref, w_all):
        pass
    own_block.wait()
    own_rows.wait()
    for copy in copies:
        copy.wait_recv()

    def chunk(owner):
        start = pl.multiple_of(lax.rem(owner, 2) * half, half)
        return back.at[lax.div(owner, 2), pl.ds(start, half)]

    own_cols = pltpu.make_async_copy(chunk(dp), cols.at[dp], local_sem.at[2])
    own_cols.start()
    arrivals = [(dp, own_cols)]
    for step in far_first(planes):
        owner = lax.rem(dp + step, planes)
        source = lax.rem(dp + planes - step, planes)
        arrivals.append((source, links.start(chunk(owner), cols.at[dp], {"dp": owner})))

    def add_head(head, carry):
        block = w_all[:, pl.ds(head, 1)].reshape(input_sum.shape[0], w_all.shape[3])
        term = jnp.dot(block, back[head], preferred_element_type=jnp.float32)
        input_sum[...] += term.astype(jnp.bfloat16).astype(jnp.float32)
        return carry

    group = 4
    for first in range(0, planes, group):
        members = arrivals[first : first + group]
        for source, copy in members:
            if copy is own_cols:
                copy.wait()
            else:
                copy.wait_recv()
        left = jnp.concatenate([cols[source] for source, _ in members], axis=1)
        right = jnp.concatenate([tokens_ref[source] for source, _ in members], axis=0)
        weight_sum[...] += jnp.dot(left, right, preferred_element_type=jnp.float32)

    mean = weight_sum[...] * (1.0 / planes)
    parts[...] = mean.T.astype(parts.dtype).reshape(parts.shape)
    add_head(0, 0)
    own_part = pltpu.make_async_copy(parts.at[dp], rows_in.at[dp], local_sem.at[0])
    own_part.start()
    copies = all_to_all_start(links, "dp", dp, planes, parts, rows_in)
    lax.fori_loop(1, 8, add_head, 0)
    own_part.wait()
    for copy in copies:
        copy.wait_recv()

    def head_rows(owner):
        return rows_in.at[pl.ds(owner * pair, pair)]

    own_head = pltpu.make_async_copy(head_rows(me), weight_ref.at[me], local_sem.at[1])
    own_head.start()
    copies = []
    for step in far_first(n):
        owner = lax.rem(me + step, n)
        copies.append(links.start(head_rows(owner), weight_ref.at[me], {"ctx": owner}))
    lax.fori_loop(8, n, add_head, 0)
    input_ref[...] = input_sum[...].T.astype(input_ref.dtype)
    own_head.wait()
    for copy in copies:
        copy.wait_recv()
    links.wait_sends()


def send_back(grad_t, w_rows, tokens_all):
    n, columns, tokens = grad_t.shape
    planes, _, width = tokens_all.shape
    rows, half = width // planes, n * columns // planes
    copies = 2 * (n - 1) + 2 * (planes - 1) + PLANE_COPIES
    bf, f32 = jnp.bfloat16, jnp.float32
    return pl.pallas_call(
        functools.partial(return_kernel, n, planes),
        out_shape=(
            jax.ShapeDtypeStruct((tokens, width), bf),
            jax.ShapeDtypeStruct((n, planes // n, rows, half), bf),
        ),
        in_specs=[VMEM, VMEM, VMEM],
        out_specs=(VMEM, VMEM),
        scratch_shapes=[
            pltpu.VMEM(grad_t.shape, bf),
            pltpu.VMEM((planes, half, tokens), bf),
            pltpu.VMEM((planes,) + w_rows.shape, bf),
            pltpu.VMEM((width, tokens), f32),
            pltpu.VMEM((half, width), f32),
            pltpu.VMEM((planes, rows, half), bf),
            pltpu.VMEM((planes, rows, half), bf),
            pltpu.SemaphoreType.DMA((copies,)),
            pltpu.SemaphoreType.DMA((copies,)),
            pltpu.SemaphoreType.DMA((3,)),
        ],
        compiler_params=pltpu.CompilerParams(
            collective_id=2, has_side_effects=True, vmem_limit_bytes=36 << 20
        ),
    )(grad_t, w_rows, tokens_all)


def body(layer_input, projected, grad_output, w_qkv, lengths, block_perm):
    tokens_dev = layer_input.shape[1]
    width = layer_input.shape[2]
    ctx_count = lax.axis_size("ctx")
    data_count = lax.axis_size("dp")
    columns = 3 * DH
    packed = jnp.concatenate(
        [
            projected[0].reshape(tokens_dev, ctx_count, columns),
            grad_output[0].reshape(tokens_dev, ctx_count, DH),
        ],
        axis=2,
    ).transpose(1, 0, 2)
    blocks, tokens_all, w_rows = gather(packed, layer_input[0], w_qkv, data_count)
    grad_t = attention(blocks, lengths, block_perm)
    grad_input, parts = send_back(grad_t, w_rows, tokens_all)
    grad_weight = jnp.sum(parts.astype(jnp.float32), axis=0).transpose(1, 0, 2)
    grad_weight = grad_weight.reshape(width // data_count, columns)
    return (grad_input[None], grad_weight)


def solution(mesh):
    return jax.shard_map(
        body,
        mesh=mesh,
        in_specs=(
            P("dp", "ctx", None),
            P("dp", "ctx", None),
            P("dp", "ctx", None),
            P("dp", "ctx"),
            P("dp", None),
            P("dp", None),
        ),
        out_specs=(P("dp", "ctx", None), P("dp", "ctx")),
        check_vma=False,
    )
```

```python
import functools

import jax
import jax.numpy as jnp
from jax import lax
from jax.experimental import pallas as pl
from jax.experimental.pallas import tpu as pltpu
from jax.sharding import PartitionSpec as P

DH = 64
BLK = 128
LAG = 5
MESH = pl.DeviceIdType.MESH
VMEM = pl.BlockSpec(memory_space=pltpu.VMEM)


def sigmoid(value):
    return 0.5 * jnp.tanh(0.5 * value) + 0.5


def attention_kernel(tile, lengths_ref, perm_ref, x_ref, out_ref, q_s, k_s, v_s, g_s, kt_s, gq_s, gk_s, gv_s, start_s, scale_s):
    slots = x_ref.shape[0]
    whole = slots * BLK
    users = lengths_ref.shape[1]
    count = whole // tile

    pos = lax.broadcasted_iota(jnp.int32, (count, tile), 0) * tile + lax.broadcasted_iota(jnp.int32, (count, tile), 1)
    first = jnp.zeros((count, tile), jnp.int32)
    length = jnp.ones((count, tile), jnp.int32)
    end = jnp.int32(0)
    for user in range(users):
        begin = end
        end = begin + lengths_ref[0, user]
        inside = pos >= begin
        first = jnp.where(inside, begin, first)
        length = jnp.where(inside, lengths_ref[0, user], length)
    start_s[...] = first
    scale_s[...] = lax.rsqrt(length.astype(jnp.float32))

    @pl.loop(0, slots, unroll=4)
    def _(slot):
        row = pl.multiple_of(perm_ref[0, slot] * BLK, BLK)
        block = x_ref[slot]
        pre = block[:, : 3 * DH].astype(jnp.float32)
        active = (pre * sigmoid(pre)).astype(jnp.bfloat16)
        q_s[pl.ds(row, BLK), :] = active[:, :DH] * jnp.bfloat16(0.0625)
        key = active[:, DH : 2 * DH]
        k_s[pl.ds(row, BLK), :] = key
        kt_s[:, pl.ds(row, BLK)] = key.T
        v_s[pl.ds(row, BLK), :] = active[:, 2 * DH :]
        g_s[pl.ds(row, BLK), :] = block[:, 3 * DH :]

    gq_s[...] = jnp.zeros_like(gq_s)
    contract = (((1,), (1,)), ((), ()))

    @pl.loop(0, count)
    def _(key_block):
        key_row = pl.multiple_of(key_block * tile, tile)
        last_key = key_row + tile - 1
        limit = jnp.int32(0)
        total = jnp.int32(0)
        for user in range(users):
            begin = total
            total = begin + lengths_ref[0, user]
            limit = jnp.where(last_key >= begin, total, limit)
        stop = (limit + tile - 1) // tile
        keys = k_s[pl.ds(key_row, tile), :]
        values = v_s[pl.ds(key_row, tile), :]
        keys_t = kt_s[:, pl.ds(key_row, tile)]
        key_pos = key_row + lax.broadcasted_iota(jnp.int32, (tile, 1), 0)

        def step(query_block, carry):
            gk, gv = carry
            query_row = pl.multiple_of(query_block * tile, tile)
            queries = q_s[pl.ds(query_row, tile), :]
            grads = g_s[pl.ds(query_row, tile), :]
            half = lax.dot_general(keys, queries, contract, preferred_element_type=jnp.float32)
            gw = lax.dot_general(values, grads, contract, preferred_element_type=jnp.float32)
            first_row = start_s[pl.ds(query_block, 1), :]
            scale_row = scale_s[pl.ds(query_block, 1), :]
            query_pos = query_row + lax.broadcasted_iota(jnp.int32, (1, tile), 1)
            visible = (key_pos >= first_row) & (key_pos <= query_pos)
            th = jnp.tanh(half)
            up = 1.0 + th
            w = half * up
            slope = up + w * (1.0 - th)
            scale = jnp.where(visible, scale_row, 0.0)
            weights = (w * scale).astype(jnp.bfloat16)
            gs = (gw * slope * scale).astype(jnp.bfloat16)
            gv = gv + jnp.dot(weights, grads, preferred_element_type=jnp.float32)
            gk = gk + jnp.dot(gs, queries, preferred_element_type=jnp.float32)
            gq_s[:, pl.ds(query_row, tile)] += jnp.dot(keys_t, gs, preferred_element_type=jnp.float32)
            return gk, gv

        zero = jnp.zeros((tile, DH), jnp.float32)
        gk, gv = lax.fori_loop(key_block, stop, step, (zero, zero))
        gk_s[pl.ds(key_row, tile), :] = gk
        gv_s[pl.ds(key_row, tile), :] = gv

    @pl.loop(0, slots, unroll=4)
    def _(slot):
        row = pl.multiple_of(perm_ref[0, slot] * BLK, BLK)
        pre = x_ref[slot][:, : 3 * DH].astype(jnp.float32)
        sigma = sigmoid(pre)
        slope = sigma * (1.0 + pre * (1.0 - sigma))
        gq = gq_s[:, pl.ds(row, BLK)].T * 0.0625
        gk = gk_s[pl.ds(row, BLK), :]
        gv = gv_s[pl.ds(row, BLK), :]
        out_ref[slot, :DH, :] = (gq * slope[:, :DH]).T.astype(jnp.bfloat16)
        out_ref[slot, DH : 2 * DH, :] = (gk * slope[:, DH : 2 * DH]).T.astype(jnp.bfloat16)
        out_ref[slot, 2 * DH :, :] = (gv * slope[:, 2 * DH :]).T.astype(jnp.bfloat16)


def attention(packed, lengths, perm, tile=256):
    slots = packed.shape[0]
    whole = slots * BLK
    vmem = pl.BlockSpec(memory_space=pltpu.VMEM)
    smem = pl.BlockSpec(memory_space=pltpu.SMEM)
    bf, f32 = jnp.bfloat16, jnp.float32
    return pl.pallas_call(
        functools.partial(attention_kernel, tile),
        out_shape=jax.ShapeDtypeStruct((slots, 3 * DH, BLK), bf),
        in_specs=[smem, smem, vmem],
        out_specs=vmem,
        scratch_shapes=[
            pltpu.VMEM((whole, DH), bf),
            pltpu.VMEM((whole, DH), bf),
            pltpu.VMEM((whole, DH), bf),
            pltpu.VMEM((whole, DH), bf),
            pltpu.VMEM((DH, whole), bf),
            pltpu.VMEM((DH, whole), f32),
            pltpu.VMEM((whole, DH), f32),
            pltpu.VMEM((whole, DH), f32),
            pltpu.VMEM((whole // tile, tile), jnp.int32),
            pltpu.VMEM((whole // tile, tile), f32),
        ],
        compiler_params=pltpu.CompilerParams(vmem_limit_bytes=24 << 20),
    )(lengths, perm, packed)


class Links:
    def __init__(self, send_sem, recv_sem):
        self.send_sem, self.recv_sem = send_sem, recv_sem
        self.copies = []

    def start(self, src, dst, device):
        k = len(self.copies)
        copy = pltpu.make_async_remote_copy(
            src_ref=src,
            dst_ref=dst,
            send_sem=self.send_sem.at[k],
            recv_sem=self.recv_sem.at[k],
            device_id=device,
            device_id_type=MESH,
        )
        copy.start()
        self.copies.append(copy)
        return copy

    def wait_sends(self):
        for copy in self.copies:
            copy.wait_send()


def far_first(n):
    order = []
    for near in range(n // 2, 0, -1):
        order += sorted({near, n - near})
    return order


def all_to_all_start(links, axis, me, n, src_ref, dst_ref):
    copies = []
    for step in far_first(n):
        peer = lax.rem(me + step, n)
        copies.append(links.start(src_ref.at[peer], dst_ref.at[me], {axis: peer}))
    return copies


def plane_gather(links, own_ref, all_ref, side=4):
    dp = lax.axis_index("dp")
    core = lax.rem(dp, 2)
    chip = lax.div(dp, 2)
    x, y = lax.rem(chip, side), lax.div(chip, side)
    a = x * (1 - core) + y * core
    b = y * (1 - core) + x * core
    partner = {"dp": dp + 1 - 2 * core}
    depth = own_ref.shape[0] // 2
    part = [pl.ds(0, depth), pl.ds(depth, depth)]

    def index(i, j):
        p, q = lax.rem(a + i + side, side), lax.rem(b + j + side, side)
        px = p * (1 - core) + q * core
        py = q * (1 - core) + p * core
        return (py * side + px) * 2 + core

    def device(i, j):
        return {"dp": index(i, j)}

    across = []

    def hand_over(i, j, src=None):
        ref = all_ref.at[index(i, j)]
        across.append(links.start(ref if src is None else src, ref, partner))

    def spread(i, src=None):
        ref = all_ref.at[index(i, 0)]
        src = ref if src is None else src
        up = links.start(src, ref, device(0, 1))
        down = links.start(src, ref, device(0, -1))
        hand_over(i, 0, src)
        return up, down

    def pass_on(i, pair):
        up, down = pair
        up.wait_recv()
        ref = all_ref.at[index(i, -1), part[1]]
        far_up = links.start(ref, ref, device(0, 1))
        hand_over(i, -1)
        down.wait_recv()
        ref = all_ref.at[index(i, 1), part[0]]
        far_down = links.start(ref, ref, device(0, -1))
        hand_over(i, 1)
        return far_up, far_down

    def finish(i, pair):
        pair[0].wait_recv()
        pair[1].wait_recv()
        hand_over(i, 2)

    own_slot = all_ref.at[index(0, 0)]
    up = links.start(own_ref, own_slot, device(1, 0))
    down = links.start(own_ref, own_slot, device(-1, 0))
    first = spread(0, own_ref)
    yield
    up.wait_recv()
    ref = all_ref.at[index(-1, 0), part[1]]
    far_up = links.start(ref, ref, device(1, 0))
    second = spread(-1)
    yield
    down.wait_recv()
    ref = all_ref.at[index(1, 0), part[0]]
    far_down = links.start(ref, ref, device(-1, 0))
    third = spread(1)
    yield
    first = pass_on(0, first)
    yield
    far_up.wait_recv()
    far_down.wait_recv()
    fourth = spread(2)
    yield
    second = pass_on(-1, second)
    yield
    third = pass_on(1, third)
    yield
    finish(0, first)
    fourth = pass_on(2, fourth)
    yield
    finish(-1, second)
    finish(1, third)
    yield
    finish(2, fourth)
    yield
    for copy in across:
        copy.wait_recv()


PLANE_COPIES = 2 + 2 + 4 * 4 + 16


def greet(axis_peers):
    barrier = pltpu.get_barrier_semaphore()
    for device in axis_peers:
        pl.semaphore_signal(barrier, inc=1, device_id=device, device_id_type=MESH)
    return barrier, len(axis_peers)


def ring_peers(me, n):
    return [{"ctx": lax.rem(me + step, n)} for step in range(1, n)]


def plane_peers(dp, planes):
    return [{"dp": lax.rem(dp + step, planes)} for step in range(1, planes)]


def gather_kernel(
    n, pre_ref, grad_ref, tokens_ref, w_ref, recv_ref, tokens_all_ref, w_rows_ref, packed_ref, send_sem, recv_sem, local_sem
):
    me = lax.axis_index("ctx")
    dp = lax.axis_index("dp")
    core = lax.rem(dp, 2)
    chip = lax.div(dp, 2)
    x, y = lax.rem(chip, 4), lax.div(chip, 4)
    peers = ring_peers(me, n)
    peers += [{"dp": dp + 1 - 2 * core}]
    peers += [{"dp": (y * 4 + lax.rem(x + step, 4)) * 2 + core} for step in (1, 3)]
    peers += [{"dp": (lax.rem(y + step, 4) * 4 + x) * 2 + core} for step in (1, 3)]
    barrier, count = greet(peers)
    links = Links(send_sem, recv_sem)
    columns = 3 * DH
    for head in range(n):
        packed_ref[head, :, :columns] = pre_ref[:, head * columns : (head + 1) * columns]
        packed_ref[head, :, columns:] = grad_ref[:, head * DH : (head + 1) * DH]
    own = [
        pltpu.make_async_copy(tokens_ref, tokens_all_ref.at[dp], local_sem.at[1]),
        pltpu.make_async_copy(w_ref, w_rows_ref.at[me], local_sem.at[2]),
    ]
    for copy in own:
        copy.start()
    pl.semaphore_wait(barrier, count)
    own.append(pltpu.make_async_copy(packed_ref.at[me], recv_ref.at[me], local_sem.at[0]))
    own[-1].start()
    plane = plane_gather(links, tokens_ref, tokens_all_ref)
    next(plane)
    copies = all_to_all_start(links, "ctx", me, n, packed_ref, recv_ref)
    for step in far_first(n):
        copies.append(links.start(w_ref, w_rows_ref.at[me], {"ctx": lax.rem(me + step, n)}))
    for _ in plane:
        pass
    for copy in copies:
        copy.wait_recv()
    links.wait_sends()
    for copy in own:
        copy.wait()


def gather(pre, grads, tokens, w, n, planes):
    copies = (n - 1) * 2 + PLANE_COPIES
    packed = (n, tokens.shape[0], 4 * DH)
    return pl.pallas_call(
        functools.partial(gather_kernel, n),
        out_shape=(
            jax.ShapeDtypeStruct(packed, pre.dtype),
            jax.ShapeDtypeStruct((planes,) + tokens.shape, tokens.dtype),
            jax.ShapeDtypeStruct((n,) + w.shape, w.dtype),
        ),
        in_specs=[VMEM, VMEM, VMEM, VMEM],
        out_specs=(VMEM, VMEM, VMEM),
        scratch_shapes=[
            pltpu.VMEM(packed, pre.dtype),
            pltpu.SemaphoreType.DMA((copies,)),
            pltpu.SemaphoreType.DMA((copies,)),
            pltpu.SemaphoreType.DMA((3,)),
        ],
        compiler_params=pltpu.CompilerParams(
            collective_id=1, has_side_effects=True, vmem_limit_bytes=24 << 20
        ),
    )(pre, grads, tokens, w)


def return_kernel(
    n, planes, grad_ref, w_rows_ref, tokens_ref, input_ref, weight_ref,
    back, cols, w_all, input_sum, weight_sum, parts, rows_in, send_sem, recv_sem, forward_send, forward_recv, local_sem,
):
    me = lax.axis_index("ctx")
    dp = lax.axis_index("dp")
    half = cols.shape[1]
    pair = planes // n
    barrier, count = greet(ring_peers(me, n) + plane_peers(dp, planes))
    own_block = pltpu.make_async_copy(grad_ref.at[me], back.at[me], local_sem.at[0])
    own_block.start()
    own_rows = pltpu.make_async_copy(w_rows_ref, w_all.at[dp], local_sem.at[1])
    own_rows.start()
    input_sum[...] = jnp.zeros_like(input_sum)
    weight_sum[...] = jnp.zeros_like(weight_sum)
    pl.semaphore_wait(barrier, count)
    links = Links(send_sem, recv_sem)
    turn = lax.rem(lax.div(dp, 2), n - 1)
    arrivals = []
    for place in range(n - 1):
        index = lax.rem(turn + place, n - 1)
        odd, near = lax.rem(index, 2), lax.div(index, 2)
        step = (near + 1) * (1 - odd) + (n - 1 - near) * odd
        peer = lax.rem(me + step, n)
        copy = links.start(grad_ref.at[peer], back.at[me], {"ctx": peer})
        arrivals.append((lax.rem(me + n - step, n), copy))

    def forward(head, place, source):
        for side in range(2):
            owner = head * 2 + side
            chunk = source.at[head, pl.ds(side * half, half)]

            def to_owner(chunk=chunk, owner=owner, side=side):
                return pltpu.make_async_remote_copy(
                    src_ref=chunk,
                    dst_ref=cols.at[dp],
                    send_sem=forward_send.at[2 * place + side],
                    recv_sem=forward_recv.at[dp],
                    device_id={"dp": owner},
                    device_id_type=MESH,
                )

            @pl.when(owner != dp)
            def _():
                to_owner().start()

            @pl.when(owner == dp)
            def _():
                pltpu.make_async_copy(chunk, cols.at[dp], forward_recv.at[dp]).start()

            sent.append((owner, to_owner))

    def add_head(head, carry):
        block = w_all[:, pl.ds(head, 1)].reshape(input_sum.shape[0], w_all.shape[3])
        term = jnp.dot(block, back[head], preferred_element_type=jnp.float32)
        input_sum[...] += term.astype(jnp.bfloat16).astype(jnp.float32)
        return carry

    ahead = lax.rem(me + n - lax.div(dp, 2), n)
    short = lax.div(n + n // 2 - ahead, n)
    own_place = short * 2 * (ahead - 1) + (1 - short) * (2 * n - 1 - 2 * ahead)

    def add_sources(first):
        sources = []
        for place in range(first, first + 2):
            chip = n - 1 if place == n - 1 else lax.rem(own_place - place + 2 * n - 2, n - 1)
            sources += [2 * chip, 2 * chip + 1]
        for source in sources:
            pltpu.make_async_copy(cols.at[source], cols.at[source], forward_recv.at[source]).wait()
        left = jnp.concatenate([cols[source] for source in sources], axis=1)
        right = jnp.concatenate([tokens_ref[source] for source in sources], axis=0)
        weight_sum[...] += jnp.dot(left, right, preferred_element_type=jnp.float32)

    sent = []
    forward(me, n - 1, grad_ref)
    plane = plane_gather(links, w_rows_ref, w_all)
    next(plane)
    added = 0
    for place, (head, copy) in enumerate(arrivals):
        copy.wait_recv()
        forward(head, place, back)
        next(plane, None)
        if place >= added + LAG and added + 1 < n:
            add_sources(added)
            added += 2
    for _ in plane:
        pass
    own_block.wait()
    own_rows.wait()
    while added < n:
        add_sources(added)
        added += 2

    mean = weight_sum[...] * (1.0 / planes)
    parts[...] = mean.T.astype(parts.dtype).reshape(parts.shape)
    add_head(0, 0)
    own_part = pltpu.make_async_copy(parts.at[dp], rows_in.at[dp], local_sem.at[0])
    own_part.start()
    copies = all_to_all_start(links, "dp", dp, planes, parts, rows_in)
    lax.fori_loop(1, 8, add_head, 0)
    own_part.wait()
    for copy in copies:
        copy.wait_recv()

    def head_rows(owner):
        return rows_in.at[pl.ds(owner * pair, pair)]

    own_head = pltpu.make_async_copy(head_rows(me), weight_ref.at[me], local_sem.at[1])
    own_head.start()
    copies = []
    for step in far_first(n):
        owner = lax.rem(me + step, n)
        copies.append(links.start(head_rows(owner), weight_ref.at[me], {"ctx": owner}))
    lax.fori_loop(8, n, add_head, 0)
    input_ref[...] = input_sum[...].T.astype(input_ref.dtype)
    own_head.wait()
    for copy in copies:
        copy.wait_recv()
    links.wait_sends()
    for owner, to_owner in sent:

        @pl.when(owner != dp)
        def _():
            to_owner().wait_send()


def send_back(grad_t, w_rows, tokens_all):
    n, columns, tokens = grad_t.shape
    planes, _, width = tokens_all.shape
    rows, half = width // planes, n * columns // planes
    copies = 2 * (n - 1) + planes - 1 + PLANE_COPIES
    bf, f32 = jnp.bfloat16, jnp.float32
    return pl.pallas_call(
        functools.partial(return_kernel, n, planes),
        out_shape=(
            jax.ShapeDtypeStruct((tokens, width), bf),
            jax.ShapeDtypeStruct((n, planes // n, rows, half), bf),
        ),
        in_specs=[VMEM, VMEM, VMEM],
        out_specs=(VMEM, VMEM),
        scratch_shapes=[
            pltpu.VMEM(grad_t.shape, bf),
            pltpu.VMEM((planes, half, tokens), bf),
            pltpu.VMEM((planes,) + w_rows.shape, bf),
            pltpu.VMEM((width, tokens), f32),
            pltpu.VMEM((half, width), f32),
            pltpu.VMEM((planes, rows, half), bf),
            pltpu.VMEM((planes, rows, half), bf),
            pltpu.SemaphoreType.DMA((copies,)),
            pltpu.SemaphoreType.DMA((copies,)),
            pltpu.SemaphoreType.DMA((2 * n,)),
            pltpu.SemaphoreType.DMA((planes,)),
            pltpu.SemaphoreType.DMA((2,)),
        ],
        compiler_params=pltpu.CompilerParams(
            collective_id=2, has_side_effects=True, vmem_limit_bytes=36 << 20
        ),
    )(grad_t, w_rows, tokens_all)


def body(layer_input, projected, grad_output, w_qkv, lengths, block_perm):
    width = layer_input.shape[2]
    ctx_count = lax.axis_size("ctx")
    data_count = lax.axis_size("dp")
    columns = 3 * DH
    blocks, tokens_all, w_rows = gather(
        projected[0], grad_output[0], layer_input[0], w_qkv, ctx_count, data_count
    )
    grad_t = attention(blocks, lengths, block_perm)
    grad_input, parts = send_back(grad_t, w_rows, tokens_all)
    grad_weight = jnp.sum(parts.astype(jnp.float32), axis=0).transpose(1, 0, 2)
    grad_weight = grad_weight.reshape(width // data_count, columns)
    return (grad_input[None], grad_weight)


def solution(mesh):
    return jax.shard_map(
        body,
        mesh=mesh,
        in_specs=(
            P("dp", "ctx", None),
            P("dp", "ctx", None),
            P("dp", "ctx", None),
            P("dp", "ctx"),
            P("dp", None),
            P("dp", None),
        ),
        out_specs=(P("dp", "ctx", None), P("dp", "ctx")),
        check_vma=False,
    )
```

```python
import functools

import jax
import jax.numpy as jnp
from jax import lax
from jax.experimental import pallas as pl
from jax.experimental.pallas import tpu as pltpu
from jax.sharding import PartitionSpec as P

DH = 64
BLK = 128
LAG = 5
MESH = pl.DeviceIdType.MESH
VMEM = pl.BlockSpec(memory_space=pltpu.VMEM)
HBM = pl.BlockSpec(memory_space=pltpu.HBM)


def sigmoid(value):
    return 0.5 * jnp.tanh(0.5 * value) + 0.5


def attention_kernel(tile, lengths_ref, perm_ref, x_ref, out_ref, q_s, k_s, v_s, g_s, kt_s, gq_s, gk_s, gv_s, start_s, scale_s):
    slots = x_ref.shape[0]
    whole = slots * BLK
    users = lengths_ref.shape[1]
    count = whole // tile

    pos = lax.broadcasted_iota(jnp.int32, (count, tile), 0) * tile + lax.broadcasted_iota(jnp.int32, (count, tile), 1)
    first = jnp.zeros((count, tile), jnp.int32)
    length = jnp.ones((count, tile), jnp.int32)
    end = jnp.int32(0)
    for user in range(users):
        begin = end
        end = begin + lengths_ref[0, user]
        inside = pos >= begin
        first = jnp.where(inside, begin, first)
        length = jnp.where(inside, lengths_ref[0, user], length)
    start_s[...] = first
    scale_s[...] = lax.rsqrt(length.astype(jnp.float32))

    @pl.loop(0, slots, unroll=4)
    def _(slot):
        row = pl.multiple_of(perm_ref[0, slot] * BLK, BLK)
        block = x_ref[slot]
        pre = block[:, : 3 * DH].astype(jnp.float32)
        active = (pre * sigmoid(pre)).astype(jnp.bfloat16)
        q_s[pl.ds(row, BLK), :] = active[:, :DH] * jnp.bfloat16(0.0625)
        key = active[:, DH : 2 * DH]
        k_s[pl.ds(row, BLK), :] = key
        kt_s[:, pl.ds(row, BLK)] = key.T
        v_s[pl.ds(row, BLK), :] = active[:, 2 * DH :]
        g_s[pl.ds(row, BLK), :] = block[:, 3 * DH :]

    gq_s[...] = jnp.zeros_like(gq_s)
    contract = (((1,), (1,)), ((), ()))

    @pl.loop(0, count)
    def _(key_block):
        key_row = pl.multiple_of(key_block * tile, tile)
        last_key = key_row + tile - 1
        limit = jnp.int32(0)
        total = jnp.int32(0)
        for user in range(users):
            begin = total
            total = begin + lengths_ref[0, user]
            limit = jnp.where(last_key >= begin, total, limit)
        stop = (limit + tile - 1) // tile
        keys = k_s[pl.ds(key_row, tile), :]
        values = v_s[pl.ds(key_row, tile), :]
        keys_t = kt_s[:, pl.ds(key_row, tile)]
        key_pos = key_row + lax.broadcasted_iota(jnp.int32, (tile, 1), 0)

        def step(query_block, carry):
            gk, gv = carry
            query_row = pl.multiple_of(query_block * tile, tile)
            queries = q_s[pl.ds(query_row, tile), :]
            grads = g_s[pl.ds(query_row, tile), :]
            half = lax.dot_general(keys, queries, contract, preferred_element_type=jnp.float32)
            gw = lax.dot_general(values, grads, contract, preferred_element_type=jnp.float32)
            first_row = start_s[pl.ds(query_block, 1), :]
            scale_row = scale_s[pl.ds(query_block, 1), :]
            query_pos = query_row + lax.broadcasted_iota(jnp.int32, (1, tile), 1)
            visible = (key_pos >= first_row) & (key_pos <= query_pos)
            th = jnp.tanh(half)
            up = 1.0 + th
            w = half * up
            slope = up + w * (1.0 - th)
            scale = jnp.where(visible, scale_row, 0.0)
            weights = (w * scale).astype(jnp.bfloat16)
            gs = (gw * slope * scale).astype(jnp.bfloat16)
            gv = gv + jnp.dot(weights, grads, preferred_element_type=jnp.float32)
            gk = gk + jnp.dot(gs, queries, preferred_element_type=jnp.float32)
            gq_s[:, pl.ds(query_row, tile)] += jnp.dot(keys_t, gs, preferred_element_type=jnp.float32)
            return gk, gv

        zero = jnp.zeros((tile, DH), jnp.float32)
        gk, gv = lax.fori_loop(key_block, stop, step, (zero, zero))
        gk_s[pl.ds(key_row, tile), :] = gk
        gv_s[pl.ds(key_row, tile), :] = gv

    @pl.loop(0, slots, unroll=4)
    def _(slot):
        row = pl.multiple_of(perm_ref[0, slot] * BLK, BLK)
        pre = x_ref[slot][:, : 3 * DH].astype(jnp.float32)
        sigma = sigmoid(pre)
        slope = sigma * (1.0 + pre * (1.0 - sigma))
        gq = gq_s[:, pl.ds(row, BLK)].T * 0.0625
        gk = gk_s[pl.ds(row, BLK), :]
        gv = gv_s[pl.ds(row, BLK), :]
        out_ref[slot, :DH, :] = (gq * slope[:, :DH]).T.astype(jnp.bfloat16)
        out_ref[slot, DH : 2 * DH, :] = (gk * slope[:, DH : 2 * DH]).T.astype(jnp.bfloat16)
        out_ref[slot, 2 * DH :, :] = (gv * slope[:, 2 * DH :]).T.astype(jnp.bfloat16)


def attention(packed, lengths, perm, tile=256):
    slots = packed.shape[0]
    whole = slots * BLK
    vmem = pl.BlockSpec(memory_space=pltpu.VMEM)
    smem = pl.BlockSpec(memory_space=pltpu.SMEM)
    bf, f32 = jnp.bfloat16, jnp.float32
    return pl.pallas_call(
        functools.partial(attention_kernel, tile),
        out_shape=jax.ShapeDtypeStruct((slots, 3 * DH, BLK), bf),
        in_specs=[smem, smem, vmem],
        out_specs=vmem,
        scratch_shapes=[
            pltpu.VMEM((whole, DH), bf),
            pltpu.VMEM((whole, DH), bf),
            pltpu.VMEM((whole, DH), bf),
            pltpu.VMEM((whole, DH), bf),
            pltpu.VMEM((DH, whole), bf),
            pltpu.VMEM((DH, whole), f32),
            pltpu.VMEM((whole, DH), f32),
            pltpu.VMEM((whole, DH), f32),
            pltpu.VMEM((whole // tile, tile), jnp.int32),
            pltpu.VMEM((whole // tile, tile), f32),
        ],
        compiler_params=pltpu.CompilerParams(vmem_limit_bytes=24 << 20),
    )(lengths, perm, packed)


class Links:
    def __init__(self, send_sem, recv_sem):
        self.send_sem, self.recv_sem = send_sem, recv_sem
        self.copies = []

    def start(self, src, dst, device):
        k = len(self.copies)
        copy = pltpu.make_async_remote_copy(
            src_ref=src,
            dst_ref=dst,
            send_sem=self.send_sem.at[k],
            recv_sem=self.recv_sem.at[k],
            device_id=device,
            device_id_type=MESH,
        )
        copy.start()
        self.copies.append(copy)
        return copy

    def wait_sends(self):
        for copy in self.copies:
            copy.wait_send()


def far_first(n):
    order = []
    for near in range(n // 2, 0, -1):
        order += sorted({near, n - near})
    return order


def all_to_all_start(links, axis, me, n, src_ref, dst_ref):
    copies = []
    for step in far_first(n):
        peer = lax.rem(me + step, n)
        copies.append(links.start(src_ref.at[peer], dst_ref.at[me], {axis: peer}))
    return copies


def plane_gather(links, own_ref, all_ref, side=4):
    dp = lax.axis_index("dp")
    core = lax.rem(dp, 2)
    chip = lax.div(dp, 2)
    x, y = lax.rem(chip, side), lax.div(chip, side)
    a = x * (1 - core) + y * core
    b = y * (1 - core) + x * core
    partner = {"dp": dp + 1 - 2 * core}
    depth = own_ref.shape[0] // 2
    part = [pl.ds(0, depth), pl.ds(depth, depth)]

    def index(i, j):
        p, q = lax.rem(a + i + side, side), lax.rem(b + j + side, side)
        px = p * (1 - core) + q * core
        py = q * (1 - core) + p * core
        return (py * side + px) * 2 + core

    def device(i, j):
        return {"dp": index(i, j)}

    across = []

    def hand_over(i, j, src=None):
        ref = all_ref.at[index(i, j)]
        across.append(links.start(ref if src is None else src, ref, partner))

    def spread(i, src=None):
        ref = all_ref.at[index(i, 0)]
        src = ref if src is None else src
        up = links.start(src, ref, device(0, 1))
        down = links.start(src, ref, device(0, -1))
        hand_over(i, 0, src)
        return up, down

    def pass_on(i, pair):
        up, down = pair
        up.wait_recv()
        ref = all_ref.at[index(i, -1), part[1]]
        far_up = links.start(ref, ref, device(0, 1))
        hand_over(i, -1)
        down.wait_recv()
        ref = all_ref.at[index(i, 1), part[0]]
        far_down = links.start(ref, ref, device(0, -1))
        hand_over(i, 1)
        return far_up, far_down

    def finish(i, pair):
        pair[0].wait_recv()
        pair[1].wait_recv()
        hand_over(i, 2)

    own_slot = all_ref.at[index(0, 0)]
    up = links.start(own_ref, own_slot, device(1, 0))
    down = links.start(own_ref, own_slot, device(-1, 0))
    first = spread(0, own_ref)
    yield
    up.wait_recv()
    ref = all_ref.at[index(-1, 0), part[1]]
    far_up = links.start(ref, ref, device(1, 0))
    second = spread(-1)
    yield
    down.wait_recv()
    ref = all_ref.at[index(1, 0), part[0]]
    far_down = links.start(ref, ref, device(-1, 0))
    third = spread(1)
    yield
    first = pass_on(0, first)
    yield
    far_up.wait_recv()
    far_down.wait_recv()
    fourth = spread(2)
    yield
    second = pass_on(-1, second)
    yield
    third = pass_on(1, third)
    yield
    finish(0, first)
    fourth = pass_on(2, fourth)
    yield
    finish(-1, second)
    finish(1, third)
    yield
    finish(2, fourth)
    yield
    for copy in across:
        copy.wait_recv()


PLANE_COPIES = 2 + 2 + 4 * 4 + 16


def greet(axis_peers):
    barrier = pltpu.get_barrier_semaphore()
    for device in axis_peers:
        pl.semaphore_signal(barrier, inc=1, device_id=device, device_id_type=MESH)
    return barrier, len(axis_peers)


def ring_peers(me, n):
    return [{"ctx": lax.rem(me + step, n)} for step in range(1, n)]


def plane_peers(dp, planes):
    return [{"dp": lax.rem(dp + step, planes)} for step in range(1, planes)]


def gather_kernel(
    n, pre_hbm, grad_hbm, tokens_ref, w_ref, recv_ref, tokens_all_ref, w_rows_ref,
    packed_ref, pre_ref, grad_ref, send_sem, recv_sem, local_sem,
):
    me = lax.axis_index("ctx")
    dp = lax.axis_index("dp")
    core = lax.rem(dp, 2)
    chip = lax.div(dp, 2)
    x, y = lax.rem(chip, 4), lax.div(chip, 4)
    peers = ring_peers(me, n)
    peers += [{"dp": dp + 1 - 2 * core}]
    peers += [{"dp": (y * 4 + lax.rem(x + step, 4)) * 2 + core} for step in (1, 3)]
    peers += [{"dp": (lax.rem(y + step, 4) * 4 + x) * 2 + core} for step in (1, 3)]
    barrier, count = greet(peers)
    links = Links(send_sem, recv_sem)
    loads = [
        pltpu.make_async_copy(pre_hbm, pre_ref, local_sem.at[3]),
        pltpu.make_async_copy(grad_hbm, grad_ref, local_sem.at[4]),
    ]
    for copy in loads:
        copy.start()
    columns = 3 * DH
    for copy in loads:
        copy.wait()
    for head in range(n):
        packed_ref[head, :, :columns] = pre_ref[:, head * columns : (head + 1) * columns]
        packed_ref[head, :, columns:] = grad_ref[:, head * DH : (head + 1) * DH]
    own = [
        pltpu.make_async_copy(tokens_ref, tokens_all_ref.at[dp], local_sem.at[1]),
        pltpu.make_async_copy(w_ref, w_rows_ref.at[me], local_sem.at[2]),
    ]
    for copy in own:
        copy.start()
    pl.semaphore_wait(barrier, count)
    own.append(pltpu.make_async_copy(packed_ref.at[me], recv_ref.at[me], local_sem.at[0]))
    own[-1].start()
    plane = plane_gather(links, tokens_ref, tokens_all_ref)
    next(plane)
    copies = all_to_all_start(links, "ctx", me, n, packed_ref, recv_ref)
    for step in far_first(n):
        copies.append(links.start(w_ref, w_rows_ref.at[me], {"ctx": lax.rem(me + step, n)}))
    for _ in plane:
        pass
    for copy in copies:
        copy.wait_recv()
    links.wait_sends()
    for copy in own:
        copy.wait()


def gather(pre, grads, tokens, w, n, planes):
    copies = (n - 1) * 2 + PLANE_COPIES
    packed = (n, tokens.shape[0], 4 * DH)
    return pl.pallas_call(
        functools.partial(gather_kernel, n),
        out_shape=(
            jax.ShapeDtypeStruct(packed, pre.dtype),
            jax.ShapeDtypeStruct((planes,) + tokens.shape, tokens.dtype),
            jax.ShapeDtypeStruct((n,) + w.shape, w.dtype),
        ),
        in_specs=[HBM, HBM, HBM, HBM],
        out_specs=(VMEM, VMEM, VMEM),
        scratch_shapes=[
            pltpu.VMEM(packed, pre.dtype),
            pltpu.VMEM(pre.shape, pre.dtype),
            pltpu.VMEM(grads.shape, grads.dtype),
            pltpu.SemaphoreType.DMA((copies,)),
            pltpu.SemaphoreType.DMA((copies,)),
            pltpu.SemaphoreType.DMA((5,)),
        ],
        compiler_params=pltpu.CompilerParams(
            collective_id=1, has_side_effects=True, vmem_limit_bytes=24 << 20
        ),
    )(*(pltpu.with_memory_space_constraint(array, pltpu.HBM) for array in (pre, grads, tokens, w)))


def push(pending, src, dst, send_sem, recv_sem, device, here):
    def remote():
        return pltpu.make_async_remote_copy(
            src_ref=src,
            dst_ref=dst,
            send_sem=send_sem,
            recv_sem=recv_sem,
            device_id=device,
            device_id_type=MESH,
        )

    @pl.when(jnp.logical_not(here))
    def _():
        remote().start()

    @pl.when(here)
    def _():
        pltpu.make_async_copy(src, dst, recv_sem).start()

    pending.append((here, remote))


def landed(ref, sem):
    pltpu.make_async_copy(ref, ref, sem).wait()


def return_kernel(
    n, planes, grad_ref, w_rows_ref, tokens_ref, input_ref, weight_ref,
    back, cols, w_all, input_sum, weight_sum, parts, rows_in, heads_in, send_sem, recv_sem,
    forward_send, forward_recv, local_sem,
):
    me = lax.axis_index("ctx")
    dp = lax.axis_index("dp")
    half = cols.shape[1]
    barrier, count = greet(ring_peers(me, n) + plane_peers(dp, planes))
    own_block = pltpu.make_async_copy(grad_ref.at[me], back.at[me], local_sem.at[0])
    own_block.start()
    own_rows = pltpu.make_async_copy(w_rows_ref, w_all.at[dp], local_sem.at[1])
    own_rows.start()
    input_sum[...] = jnp.zeros_like(input_sum)
    weight_sum[...] = jnp.zeros_like(weight_sum)
    pl.semaphore_wait(barrier, count)
    links = Links(send_sem, recv_sem)
    turn = lax.rem(lax.div(dp, 2), n - 1)
    arrivals = []
    for place in range(n - 1):
        index = lax.rem(turn + place, n - 1)
        odd, near = lax.rem(index, 2), lax.div(index, 2)
        step = (near + 1) * (1 - odd) + (n - 1 - near) * odd
        peer = lax.rem(me + step, n)
        copy = links.start(grad_ref.at[peer], back.at[me], {"ctx": peer})
        arrivals.append((lax.rem(me + n - step, n), copy))

    def forward(head, place, source):
        for side in range(2):
            owner = head * 2 + side
            push(
                pending, source.at[head, pl.ds(side * half, half)], cols.at[dp],
                forward_send.at[2 * place + side], forward_recv.at[dp], {"dp": owner}, owner == dp,
            )

    def add_head(head, carry):
        block = w_all[:, pl.ds(head, 1)].reshape(input_sum.shape[0], w_all.shape[3])
        term = jnp.dot(block, back[head], preferred_element_type=jnp.float32)
        input_sum[...] += term.astype(jnp.bfloat16).astype(jnp.float32)
        return carry

    ahead = lax.rem(me + n - lax.div(dp, 2), n)
    short = lax.div(n + n // 2 - ahead, n)
    own_place = short * 2 * (ahead - 1) + (1 - short) * (2 * n - 1 - 2 * ahead)

    def add_sources(first):
        sources = []
        for place in range(first, first + 2):
            chip = n - 1 if place == n - 1 else lax.rem(own_place - place + 2 * n - 2, n - 1)
            sources += [2 * chip, 2 * chip + 1]
        for source in sources:
            landed(cols.at[source], forward_recv.at[source])
        left = jnp.concatenate([cols[source] for source in sources], axis=1)
        right = jnp.concatenate([tokens_ref[source] for source in sources], axis=0)
        weight_sum[...] += jnp.dot(left, right, preferred_element_type=jnp.float32)

    pending = []
    forward(me, n - 1, grad_ref)
    plane = plane_gather(links, w_rows_ref, w_all)
    next(plane)
    added = 0
    for place, (head, copy) in enumerate(arrivals):
        copy.wait_recv()
        forward(head, place, back)
        next(plane, None)
        if place >= added + LAG and added + 1 < n:
            add_sources(added)
            added += 2
    own_block.wait()
    while added < n:
        add_sources(added)
        added += 2

    mean = weight_sum[...] * (1.0 / planes)
    parts[...] = mean.T.astype(parts.dtype).reshape(parts.shape)
    next(plane, None)
    own_part = pltpu.make_async_copy(parts.at[dp], rows_in.at[dp], local_sem.at[0])
    own_part.start()
    copies = all_to_all_start(links, "dp", dp, planes, parts, rows_in)
    for _ in plane:
        pass
    own_rows.wait()
    lax.fori_loop(0, 8, add_head, 0)
    own_part.wait()
    for copy in copies:
        copy.wait_recv()

    def head_rows(owner):
        return rows_in.at[pl.ds(owner * 2, 2)]

    own_head = pltpu.make_async_copy(head_rows(me), heads_in.at[me], local_sem.at[1])
    own_head.start()
    copies = []
    for step in far_first(n):
        owner = lax.rem(me + step, n)
        copies.append(links.start(head_rows(owner), heads_in.at[me], {"ctx": owner}))
    lax.fori_loop(8, n, add_head, 0)
    input_ref[...] = input_sum[...].T.astype(input_ref.dtype)
    own_head.wait()
    for copy in copies:
        copy.wait_recv()
    total = jnp.zeros(heads_in.shape[1:], jnp.float32)
    for source in range(n):
        total = total + heads_in[source].astype(jnp.float32)
    weight_ref[:, :half] = total[0]
    weight_ref[:, half:] = total[1]
    links.wait_sends()
    for here, remote in pending:

        @pl.when(jnp.logical_not(here))
        def _():
            remote().wait_send()


def send_back(grad_t, w_rows, tokens_all):
    n, columns, tokens = grad_t.shape
    planes, _, width = tokens_all.shape
    rows, half = width // planes, n * columns // planes
    copies = 2 * (n - 1) + planes - 1 + PLANE_COPIES
    bf, f32 = jnp.bfloat16, jnp.float32
    return pl.pallas_call(
        functools.partial(return_kernel, n, planes),
        out_shape=(
            jax.ShapeDtypeStruct((tokens, width), bf),
            jax.ShapeDtypeStruct((rows, columns), f32),
        ),
        in_specs=[VMEM, VMEM, VMEM],
        out_specs=(VMEM, VMEM),
        scratch_shapes=[
            pltpu.VMEM(grad_t.shape, bf),
            pltpu.VMEM((planes, half, tokens), bf),
            pltpu.VMEM((planes,) + w_rows.shape, bf),
            pltpu.VMEM((width, tokens), f32),
            pltpu.VMEM((half, width), f32),
            pltpu.VMEM((planes, rows, half), bf),
            pltpu.VMEM((planes, rows, half), bf),
            pltpu.VMEM((n, planes // n, rows, half), bf),
            pltpu.SemaphoreType.DMA((copies,)),
            pltpu.SemaphoreType.DMA((copies,)),
            pltpu.SemaphoreType.DMA((2 * n,)),
            pltpu.SemaphoreType.DMA((planes,)),
            pltpu.SemaphoreType.DMA((2,)),
        ],
        compiler_params=pltpu.CompilerParams(
            collective_id=2, has_side_effects=True, vmem_limit_bytes=36 << 20
        ),
    )(grad_t, w_rows, tokens_all)


def body(layer_input, projected, grad_output, w_qkv, lengths, block_perm):
    ctx_count = lax.axis_size("ctx")
    data_count = lax.axis_size("dp")
    blocks, tokens_all, w_rows = gather(
        projected[0], grad_output[0], layer_input[0], w_qkv, ctx_count, data_count
    )
    grad_t = attention(blocks, lengths, block_perm)
    grad_input, grad_weight = send_back(grad_t, w_rows, tokens_all)
    return (grad_input[None], grad_weight)


def solution(mesh):
    return jax.shard_map(
        body,
        mesh=mesh,
        in_specs=(
            P("dp", "ctx", None),
            P("dp", "ctx", None),
            P("dp", "ctx", None),
            P("dp", "ctx"),
            P("dp", None),
            P("dp", None),
        ),
        out_specs=(P("dp", "ctx", None), P("dp", "ctx")),
        check_vma=False,
    )
```

```python
import functools

import jax
import jax.numpy as jnp
from jax import lax
from jax.experimental import pallas as pl
from jax.experimental.pallas import tpu as pltpu
from jax.sharding import PartitionSpec as P

DH = 64
BLK = 128
LAG = 5
MESH = pl.DeviceIdType.MESH
VMEM = pl.BlockSpec(memory_space=pltpu.VMEM)
HBM = pl.BlockSpec(memory_space=pltpu.HBM)


def sigmoid(value):
    return 0.5 * jnp.tanh(0.5 * value) + 0.5


def attention_kernel(tile, lengths_hbm, perm_hbm, x_ref, out_ref, q_s, k_s, v_s, g_s, kt_s, gq_s, gk_s, gv_s, start_s, scale_s, lengths_ref, perm_ref, sem):
    loads = [
        pltpu.make_async_copy(lengths_hbm, lengths_ref, sem.at[0]),
        pltpu.make_async_copy(perm_hbm, perm_ref, sem.at[1]),
    ]
    for copy in loads:
        copy.start()
    for copy in loads:
        copy.wait()
    slots = x_ref.shape[0]
    whole = slots * BLK
    users = lengths_ref.shape[1]
    count = whole // tile

    pos = lax.broadcasted_iota(jnp.int32, (count, tile), 0) * tile + lax.broadcasted_iota(jnp.int32, (count, tile), 1)
    first = jnp.zeros((count, tile), jnp.int32)
    length = jnp.ones((count, tile), jnp.int32)
    end = jnp.int32(0)
    for user in range(users):
        begin = end
        end = begin + lengths_ref[0, user]
        inside = pos >= begin
        first = jnp.where(inside, begin, first)
        length = jnp.where(inside, lengths_ref[0, user], length)
    start_s[...] = first
    scale_s[...] = lax.rsqrt(length.astype(jnp.float32))

    @pl.loop(0, slots, unroll=8)
    def _(slot):
        row = pl.multiple_of(perm_ref[0, slot] * BLK, BLK)
        block = x_ref[slot]
        pre = block[:, : 3 * DH].astype(jnp.float32)
        active = (pre * sigmoid(pre)).astype(jnp.bfloat16)
        q_s[pl.ds(row, BLK), :] = active[:, :DH] * jnp.bfloat16(0.0625)
        key = active[:, DH : 2 * DH]
        k_s[pl.ds(row, BLK), :] = key
        kt_s[:, pl.ds(row, BLK)] = key.T
        v_s[pl.ds(row, BLK), :] = active[:, 2 * DH :]
        g_s[pl.ds(row, BLK), :] = block[:, 3 * DH :]

    gq_s[...] = jnp.zeros_like(gq_s)
    contract = (((1,), (1,)), ((), ()))

    @pl.loop(0, count)
    def _(key_block):
        key_row = pl.multiple_of(key_block * tile, tile)
        last_key = key_row + tile - 1
        limit = jnp.int32(0)
        total = jnp.int32(0)
        for user in range(users):
            begin = total
            total = begin + lengths_ref[0, user]
            limit = jnp.where(last_key >= begin, total, limit)
        stop = (limit + tile - 1) // tile
        keys = k_s[pl.ds(key_row, tile), :]
        values = v_s[pl.ds(key_row, tile), :]
        keys_t = kt_s[:, pl.ds(key_row, tile)]
        key_pos = key_row + lax.broadcasted_iota(jnp.int32, (tile, 1), 0)

        def step(query_block, carry):
            gk, gv = carry
            query_row = pl.multiple_of(query_block * tile, tile)
            queries = q_s[pl.ds(query_row, tile), :]
            grads = g_s[pl.ds(query_row, tile), :]
            half = lax.dot_general(keys, queries, contract, preferred_element_type=jnp.float32)
            gw = lax.dot_general(values, grads, contract, preferred_element_type=jnp.float32)
            first_row = start_s[pl.ds(query_block, 1), :]
            scale_row = scale_s[pl.ds(query_block, 1), :]
            query_pos = query_row + lax.broadcasted_iota(jnp.int32, (1, tile), 1)
            visible = (key_pos >= first_row) & (key_pos <= query_pos)
            th = jnp.tanh(half)
            up = 1.0 + th
            w = half * up
            slope = up + w * (1.0 - th)
            scale = jnp.where(visible, scale_row, 0.0)
            weights = (w * scale).astype(jnp.bfloat16)
            gs = (gw * slope * scale).astype(jnp.bfloat16)
            gv = gv + jnp.dot(weights, grads, preferred_element_type=jnp.float32)
            gk = gk + jnp.dot(gs, queries, preferred_element_type=jnp.float32)
            gq_s[:, pl.ds(query_row, tile)] += jnp.dot(keys_t, gs, preferred_element_type=jnp.float32)
            return gk, gv

        zero = jnp.zeros((tile, DH), jnp.float32)
        gk, gv = lax.fori_loop(key_block, stop, step, (zero, zero))
        gk_s[pl.ds(key_row, tile), :] = gk
        gv_s[pl.ds(key_row, tile), :] = gv

    @pl.loop(0, slots, unroll=8)
    def _(slot):
        row = pl.multiple_of(perm_ref[0, slot] * BLK, BLK)
        pre = x_ref[slot][:, : 3 * DH].astype(jnp.float32)
        sigma = sigmoid(pre)
        slope = sigma * (1.0 + pre * (1.0 - sigma))
        gq = gq_s[:, pl.ds(row, BLK)].T * 0.0625
        gk = gk_s[pl.ds(row, BLK), :]
        gv = gv_s[pl.ds(row, BLK), :]
        out_ref[slot, :DH, :] = (gq * slope[:, :DH]).T.astype(jnp.bfloat16)
        out_ref[slot, DH : 2 * DH, :] = (gk * slope[:, DH : 2 * DH]).T.astype(jnp.bfloat16)
        out_ref[slot, 2 * DH :, :] = (gv * slope[:, 2 * DH :]).T.astype(jnp.bfloat16)


def attention(packed, lengths, perm, tile=256):
    slots = packed.shape[0]
    whole = slots * BLK
    vmem = pl.BlockSpec(memory_space=pltpu.VMEM)
    hbm = pl.BlockSpec(memory_space=pltpu.HBM)
    lengths, perm = (pltpu.with_memory_space_constraint(array, pltpu.HBM) for array in (lengths, perm))
    bf, f32 = jnp.bfloat16, jnp.float32
    return pl.pallas_call(
        functools.partial(attention_kernel, tile),
        out_shape=jax.ShapeDtypeStruct((slots, 3 * DH, BLK), bf),
        in_specs=[hbm, hbm, vmem],
        out_specs=vmem,
        scratch_shapes=[
            pltpu.VMEM((whole, DH), bf),
            pltpu.VMEM((whole, DH), bf),
            pltpu.VMEM((whole, DH), bf),
            pltpu.VMEM((whole, DH), bf),
            pltpu.VMEM((DH, whole), bf),
            pltpu.VMEM((DH, whole), f32),
            pltpu.VMEM((whole, DH), f32),
            pltpu.VMEM((whole, DH), f32),
            pltpu.VMEM((whole // tile, tile), jnp.int32),
            pltpu.VMEM((whole // tile, tile), f32),
            pltpu.SMEM(lengths.shape, jnp.int32),
            pltpu.SMEM(perm.shape, jnp.int32),
            pltpu.SemaphoreType.DMA((2,)),
        ],
        compiler_params=pltpu.CompilerParams(vmem_limit_bytes=24 << 20),
    )(lengths, perm, packed)


class Links:
    def __init__(self, send_sem, recv_sem):
        self.send_sem, self.recv_sem = send_sem, recv_sem
        self.copies = []

    def start(self, src, dst, device):
        k = len(self.copies)
        copy = pltpu.make_async_remote_copy(
            src_ref=src,
            dst_ref=dst,
            send_sem=self.send_sem.at[k],
            recv_sem=self.recv_sem.at[k],
            device_id=device,
            device_id_type=MESH,
        )
        copy.start()
        self.copies.append(copy)
        return copy

    def wait_sends(self):
        for copy in self.copies:
            copy.wait_send()


def far_first(n):
    order = []
    for near in range(n // 2, 0, -1):
        order += sorted({near, n - near})
    return order


def all_to_all_start(links, axis, me, n, src_ref, dst_ref):
    copies = []
    for step in far_first(n):
        peer = lax.rem(me + step, n)
        copies.append(links.start(src_ref.at[peer], dst_ref.at[me], {axis: peer}))
    return copies


def plane_gather(links, own_ref, all_ref, side=4):
    dp = lax.axis_index("dp")
    core = lax.rem(dp, 2)
    chip = lax.div(dp, 2)
    x, y = lax.rem(chip, side), lax.div(chip, side)
    a = x * (1 - core) + y * core
    b = y * (1 - core) + x * core
    partner = {"dp": dp + 1 - 2 * core}
    depth = own_ref.shape[0] // 2
    part = [pl.ds(0, depth), pl.ds(depth, depth)]

    def index(i, j):
        p, q = lax.rem(a + i + side, side), lax.rem(b + j + side, side)
        px = p * (1 - core) + q * core
        py = q * (1 - core) + p * core
        return (py * side + px) * 2 + core

    def device(i, j):
        return {"dp": index(i, j)}

    across = []

    def hand_over(i, j, src=None):
        ref = all_ref.at[index(i, j)]
        across.append(links.start(ref if src is None else src, ref, partner))

    def spread(i, src=None):
        ref = all_ref.at[index(i, 0)]
        src = ref if src is None else src
        up = links.start(src, ref, device(0, 1))
        down = links.start(src, ref, device(0, -1))
        hand_over(i, 0, src)
        return up, down

    def pass_on(i, pair):
        up, down = pair
        up.wait_recv()
        ref = all_ref.at[index(i, -1), part[1]]
        far_up = links.start(ref, ref, device(0, 1))
        hand_over(i, -1)
        down.wait_recv()
        ref = all_ref.at[index(i, 1), part[0]]
        far_down = links.start(ref, ref, device(0, -1))
        hand_over(i, 1)
        return far_up, far_down

    def finish(i, pair):
        pair[0].wait_recv()
        pair[1].wait_recv()
        hand_over(i, 2)

    own_slot = all_ref.at[index(0, 0)]
    up = links.start(own_ref, own_slot, device(1, 0))
    down = links.start(own_ref, own_slot, device(-1, 0))
    first = spread(0, own_ref)
    yield
    up.wait_recv()
    ref = all_ref.at[index(-1, 0), part[1]]
    far_up = links.start(ref, ref, device(1, 0))
    second = spread(-1)
    yield
    down.wait_recv()
    ref = all_ref.at[index(1, 0), part[0]]
    far_down = links.start(ref, ref, device(-1, 0))
    third = spread(1)
    yield
    first = pass_on(0, first)
    yield
    far_up.wait_recv()
    far_down.wait_recv()
    fourth = spread(2)
    yield
    second = pass_on(-1, second)
    yield
    third = pass_on(1, third)
    yield
    finish(0, first)
    fourth = pass_on(2, fourth)
    yield
    finish(-1, second)
    finish(1, third)
    yield
    finish(2, fourth)
    yield
    for copy in across:
        copy.wait_recv()


PLANE_COPIES = 2 + 2 + 4 * 4 + 16


def greet(axis_peers):
    barrier = pltpu.get_barrier_semaphore()
    for device in axis_peers:
        pl.semaphore_signal(barrier, inc=1, device_id=device, device_id_type=MESH)
    return barrier, len(axis_peers)


def ring_peers(me, n):
    return [{"ctx": lax.rem(me + step, n)} for step in range(1, n)]


def plane_peers(dp, planes):
    return [{"dp": lax.rem(dp + step, planes)} for step in range(1, planes)]


def gather_kernel(
    n, pre_hbm, grad_hbm, tokens_ref, w_ref, recv_ref, tokens_all_ref, w_rows_ref,
    packed_ref, pre_ref, grad_ref, send_sem, recv_sem, local_sem,
):
    me = lax.axis_index("ctx")
    dp = lax.axis_index("dp")
    core = lax.rem(dp, 2)
    chip = lax.div(dp, 2)
    x, y = lax.rem(chip, 4), lax.div(chip, 4)
    peers = ring_peers(me, n)
    peers += [{"dp": dp + 1 - 2 * core}]
    peers += [{"dp": (y * 4 + lax.rem(x + step, 4)) * 2 + core} for step in (1, 3)]
    peers += [{"dp": (lax.rem(y + step, 4) * 4 + x) * 2 + core} for step in (1, 3)]
    barrier, count = greet(peers)
    links = Links(send_sem, recv_sem)
    loads = [
        pltpu.make_async_copy(pre_hbm, pre_ref, local_sem.at[3]),
        pltpu.make_async_copy(grad_hbm, grad_ref, local_sem.at[4]),
    ]
    for copy in loads:
        copy.start()
    columns = 3 * DH
    for copy in loads:
        copy.wait()
    for head in range(n):
        packed_ref[head, :, :columns] = pre_ref[:, head * columns : (head + 1) * columns]
        packed_ref[head, :, columns:] = grad_ref[:, head * DH : (head + 1) * DH]
    own = [
        pltpu.make_async_copy(tokens_ref, tokens_all_ref.at[dp], local_sem.at[1]),
        pltpu.make_async_copy(w_ref, w_rows_ref.at[me], local_sem.at[2]),
    ]
    for copy in own:
        copy.start()
    pl.semaphore_wait(barrier, count)
    own.append(pltpu.make_async_copy(packed_ref.at[me], recv_ref.at[me], local_sem.at[0]))
    own[-1].start()
    plane = plane_gather(links, tokens_ref, tokens_all_ref)
    next(plane)
    copies = all_to_all_start(links, "ctx", me, n, packed_ref, recv_ref)
    for step in far_first(n):
        copies.append(links.start(w_ref, w_rows_ref.at[me], {"ctx": lax.rem(me + step, n)}))
    for _ in plane:
        pass
    for copy in copies:
        copy.wait_recv()
    links.wait_sends()
    for copy in own:
        copy.wait()


def gather(pre, grads, tokens, w, n, planes):
    copies = (n - 1) * 2 + PLANE_COPIES
    packed = (n, tokens.shape[0], 4 * DH)
    return pl.pallas_call(
        functools.partial(gather_kernel, n),
        out_shape=(
            jax.ShapeDtypeStruct(packed, pre.dtype),
            jax.ShapeDtypeStruct((planes,) + tokens.shape, tokens.dtype),
            jax.ShapeDtypeStruct((n,) + w.shape, w.dtype),
        ),
        in_specs=[HBM, HBM, HBM, HBM],
        out_specs=(VMEM, VMEM, VMEM),
        scratch_shapes=[
            pltpu.VMEM(packed, pre.dtype),
            pltpu.VMEM(pre.shape, pre.dtype),
            pltpu.VMEM(grads.shape, grads.dtype),
            pltpu.SemaphoreType.DMA((copies,)),
            pltpu.SemaphoreType.DMA((copies,)),
            pltpu.SemaphoreType.DMA((5,)),
        ],
        compiler_params=pltpu.CompilerParams(
            collective_id=1, has_side_effects=True, vmem_limit_bytes=24 << 20
        ),
    )(*(pltpu.with_memory_space_constraint(array, pltpu.HBM) for array in (pre, grads, tokens, w)))


def push(pending, src, dst, send_sem, recv_sem, device, here):
    def remote():
        return pltpu.make_async_remote_copy(
            src_ref=src,
            dst_ref=dst,
            send_sem=send_sem,
            recv_sem=recv_sem,
            device_id=device,
            device_id_type=MESH,
        )

    @pl.when(jnp.logical_not(here))
    def _():
        remote().start()

    @pl.when(here)
    def _():
        pltpu.make_async_copy(src, dst, recv_sem).start()

    pending.append((here, remote))


def landed(ref, sem):
    pltpu.make_async_copy(ref, ref, sem).wait()


def return_kernel(
    n, planes, grad_ref, w_rows_ref, tokens_ref, input_ref, weight_ref,
    back, cols, w_all, input_sum, weight_sum, parts, rows_in, heads_in, send_sem, recv_sem,
    forward_send, forward_recv, local_sem,
):
    me = lax.axis_index("ctx")
    dp = lax.axis_index("dp")
    half = cols.shape[1]
    barrier, count = greet(ring_peers(me, n) + plane_peers(dp, planes))
    own_block = pltpu.make_async_copy(grad_ref.at[me], back.at[me], local_sem.at[0])
    own_block.start()
    own_rows = pltpu.make_async_copy(w_rows_ref, w_all.at[dp], local_sem.at[1])
    own_rows.start()
    input_sum[...] = jnp.zeros_like(input_sum)
    weight_sum[...] = jnp.zeros_like(weight_sum)
    pl.semaphore_wait(barrier, count)
    links = Links(send_sem, recv_sem)
    turn = lax.rem(lax.div(dp, 2), n - 1)
    arrivals = []
    for place in range(n - 1):
        index = lax.rem(turn + place, n - 1)
        odd, near = lax.rem(index, 2), lax.div(index, 2)
        step = (near + 1) * (1 - odd) + (n - 1 - near) * odd
        peer = lax.rem(me + step, n)
        copy = links.start(grad_ref.at[peer], back.at[me], {"ctx": peer})
        arrivals.append((lax.rem(me + n - step, n), copy))

    def forward(head, place, source):
        for side in range(2):
            owner = head * 2 + side
            push(
                pending, source.at[head, pl.ds(side * half, half)], cols.at[dp],
                forward_send.at[2 * place + side], forward_recv.at[dp], {"dp": owner}, owner == dp,
            )

    def add_head(head, carry):
        block = w_all[:, pl.ds(head, 1)].reshape(input_sum.shape[0], w_all.shape[3])
        term = jnp.dot(block, back[head], preferred_element_type=jnp.float32)
        input_sum[...] += term.astype(jnp.bfloat16).astype(jnp.float32)
        return carry

    ahead = lax.rem(me + n - lax.div(dp, 2), n)
    short = lax.div(n + n // 2 - ahead, n)
    own_place = short * 2 * (ahead - 1) + (1 - short) * (2 * n - 1 - 2 * ahead)

    def add_sources(first):
        sources = []
        for place in range(first, first + 2):
            chip = n - 1 if place == n - 1 else lax.rem(own_place - place + 2 * n - 2, n - 1)
            sources += [2 * chip, 2 * chip + 1]
        for source in sources:
            landed(cols.at[source], forward_recv.at[source])
        left = jnp.concatenate([cols[source] for source in sources], axis=1)
        right = jnp.concatenate([tokens_ref[source] for source in sources], axis=0)
        weight_sum[...] += jnp.dot(left, right, preferred_element_type=jnp.float32)

    pending = []
    forward(me, n - 1, grad_ref)
    plane = plane_gather(links, w_rows_ref, w_all)
    for _ in range(5):
        next(plane, None)
    added = 0
    for place, (head, copy) in enumerate(arrivals):
        copy.wait_recv()
        forward(head, place, back)
        next(plane, None)
        if place >= added + LAG and added + 1 < n:
            add_sources(added)
            added += 2
    own_block.wait()
    while added < n:
        add_sources(added)
        added += 2

    mean = weight_sum[...] * (1.0 / planes)
    parts[...] = mean.T.astype(parts.dtype).reshape(parts.shape)
    next(plane, None)
    own_part = pltpu.make_async_copy(parts.at[dp], rows_in.at[dp], local_sem.at[0])
    own_part.start()
    copies = all_to_all_start(links, "dp", dp, planes, parts, rows_in)
    for _ in plane:
        pass
    own_rows.wait()
    lax.fori_loop(0, 8, add_head, 0)
    own_part.wait()
    for copy in copies:
        copy.wait_recv()

    def head_rows(owner):
        return rows_in.at[pl.ds(owner * 2, 2)]

    own_head = pltpu.make_async_copy(head_rows(me), heads_in.at[me], local_sem.at[1])
    own_head.start()
    copies = []
    for step in far_first(n):
        owner = lax.rem(me + step, n)
        copies.append(links.start(head_rows(owner), heads_in.at[me], {"ctx": owner}))
    lax.fori_loop(8, n, add_head, 0)
    input_ref[...] = input_sum[...].T.astype(input_ref.dtype)
    own_head.wait()
    for copy in copies:
        copy.wait_recv()
    total = jnp.zeros(heads_in.shape[1:], jnp.float32)
    for source in range(n):
        total = total + heads_in[source].astype(jnp.float32)
    weight_ref[:, :half] = total[0]
    weight_ref[:, half:] = total[1]
    links.wait_sends()
    for here, remote in pending:

        @pl.when(jnp.logical_not(here))
        def _():
            remote().wait_send()


def send_back(grad_t, w_rows, tokens_all):
    n, columns, tokens = grad_t.shape
    planes, _, width = tokens_all.shape
    rows, half = width // planes, n * columns // planes
    copies = 2 * (n - 1) + planes - 1 + PLANE_COPIES
    bf, f32 = jnp.bfloat16, jnp.float32
    return pl.pallas_call(
        functools.partial(return_kernel, n, planes),
        out_shape=(
            jax.ShapeDtypeStruct((tokens, width), bf),
            jax.ShapeDtypeStruct((rows, columns), f32),
        ),
        in_specs=[VMEM, VMEM, VMEM],
        out_specs=(VMEM, VMEM),
        scratch_shapes=[
            pltpu.VMEM(grad_t.shape, bf),
            pltpu.VMEM((planes, half, tokens), bf),
            pltpu.VMEM((planes,) + w_rows.shape, bf),
            pltpu.VMEM((width, tokens), f32),
            pltpu.VMEM((half, width), f32),
            pltpu.VMEM((planes, rows, half), bf),
            pltpu.VMEM((planes, rows, half), bf),
            pltpu.VMEM((n, planes // n, rows, half), bf),
            pltpu.SemaphoreType.DMA((copies,)),
            pltpu.SemaphoreType.DMA((copies,)),
            pltpu.SemaphoreType.DMA((2 * n,)),
            pltpu.SemaphoreType.DMA((planes,)),
            pltpu.SemaphoreType.DMA((2,)),
        ],
        compiler_params=pltpu.CompilerParams(
            collective_id=2, has_side_effects=True, vmem_limit_bytes=36 << 20
        ),
    )(grad_t, w_rows, tokens_all)


def body(layer_input, projected, grad_output, w_qkv, lengths, block_perm):
    ctx_count = lax.axis_size("ctx")
    data_count = lax.axis_size("dp")
    blocks, tokens_all, w_rows = gather(
        projected[0], grad_output[0], layer_input[0], w_qkv, ctx_count, data_count
    )
    grad_t = attention(blocks, lengths, block_perm)
    grad_input, grad_weight = send_back(grad_t, w_rows, tokens_all)
    return (grad_input[None], grad_weight)


def solution(mesh):
    return jax.shard_map(
        body,
        mesh=mesh,
        in_specs=(
            P("dp", "ctx", None),
            P("dp", "ctx", None),
            P("dp", "ctx", None),
            P("dp", "ctx"),
            P("dp", None),
            P("dp", None),
        ),
        out_specs=(P("dp", "ctx", None), P("dp", "ctx")),
        check_vma=False,
    )
```

```python
import functools

import jax
import jax.numpy as jnp
from jax import lax
from jax.experimental import pallas as pl
from jax.experimental.pallas import tpu as pltpu
from jax.sharding import PartitionSpec as P

DH = 64
BLK = 128
LAG = 3
MESH = pl.DeviceIdType.MESH
VMEM = pl.BlockSpec(memory_space=pltpu.VMEM)
HBM = pl.BlockSpec(memory_space=pltpu.HBM)


def sigmoid(value):
    return 0.5 * jnp.tanh(0.5 * value) + 0.5


def attention_kernel(tile, lengths_hbm, perm_hbm, x_ref, out_ref, q_s, k_s, v_s, g_s, kt_s, gq_s, gk_s, gv_s, start_s, scale_s, lengths_ref, perm_ref, sem):
    loads = [
        pltpu.make_async_copy(lengths_hbm, lengths_ref, sem.at[0]),
        pltpu.make_async_copy(perm_hbm, perm_ref, sem.at[1]),
    ]
    for copy in loads:
        copy.start()
    for copy in loads:
        copy.wait()
    slots = x_ref.shape[0]
    whole = slots * BLK
    users = lengths_ref.shape[1]
    count = whole // tile

    pos = lax.broadcasted_iota(jnp.int32, (count, tile), 0) * tile + lax.broadcasted_iota(jnp.int32, (count, tile), 1)
    first = jnp.zeros((count, tile), jnp.int32)
    length = jnp.ones((count, tile), jnp.int32)
    end = jnp.int32(0)
    for user in range(users):
        begin = end
        end = begin + lengths_ref[0, user]
        inside = pos >= begin
        first = jnp.where(inside, begin, first)
        length = jnp.where(inside, lengths_ref[0, user], length)
    start_s[...] = first
    scale_s[...] = lax.rsqrt(length.astype(jnp.float32))

    @pl.loop(0, slots, unroll=8)
    def _(slot):
        row = pl.multiple_of(perm_ref[0, slot] * BLK, BLK)
        block = x_ref[slot]
        pre = block[:, : 3 * DH].astype(jnp.float32)
        active = (pre * sigmoid(pre)).astype(jnp.bfloat16)
        q_s[pl.ds(row, BLK), :] = active[:, :DH] * jnp.bfloat16(0.0625)
        key = active[:, DH : 2 * DH]
        k_s[pl.ds(row, BLK), :] = key
        kt_s[:, pl.ds(row, BLK)] = key.T
        v_s[pl.ds(row, BLK), :] = active[:, 2 * DH :]
        g_s[pl.ds(row, BLK), :] = block[:, 3 * DH :]

    gq_s[...] = jnp.zeros_like(gq_s)
    contract = (((1,), (1,)), ((), ()))

    @pl.loop(0, count)
    def _(key_block):
        key_row = pl.multiple_of(key_block * tile, tile)
        last_key = key_row + tile - 1
        limit = jnp.int32(0)
        total = jnp.int32(0)
        for user in range(users):
            begin = total
            total = begin + lengths_ref[0, user]
            limit = jnp.where(last_key >= begin, total, limit)
        stop = (limit + tile - 1) // tile
        keys = k_s[pl.ds(key_row, tile), :]
        values = v_s[pl.ds(key_row, tile), :]
        keys_t = kt_s[:, pl.ds(key_row, tile)]
        key_pos = key_row + lax.broadcasted_iota(jnp.int32, (tile, 1), 0)

        def step(query_block, carry):
            gk, gv = carry
            query_row = pl.multiple_of(query_block * tile, tile)
            queries = q_s[pl.ds(query_row, tile), :]
            grads = g_s[pl.ds(query_row, tile), :]
            half = lax.dot_general(keys, queries, contract, preferred_element_type=jnp.float32)
            gw = lax.dot_general(values, grads, contract, preferred_element_type=jnp.float32)
            first_row = start_s[pl.ds(query_block, 1), :]
            scale_row = scale_s[pl.ds(query_block, 1), :]
            query_pos = query_row + lax.broadcasted_iota(jnp.int32, (1, tile), 1)
            visible = (key_pos >= first_row) & (key_pos <= query_pos)
            th = jnp.tanh(half)
            up = 1.0 + th
            w = half * up
            slope = up + w * (1.0 - th)
            scale = jnp.where(visible, scale_row, 0.0)
            weights = (w * scale).astype(jnp.bfloat16)
            gs = (gw * slope * scale).astype(jnp.bfloat16)
            gv = gv + jnp.dot(weights, grads, preferred_element_type=jnp.float32)
            gk = gk + jnp.dot(gs, queries, preferred_element_type=jnp.float32)
            gq_s[:, pl.ds(query_row, tile)] += jnp.dot(keys_t, gs, preferred_element_type=jnp.float32)
            return gk, gv

        zero = jnp.zeros((tile, DH), jnp.float32)
        gk, gv = lax.fori_loop(key_block, stop, step, (zero, zero))
        gk_s[pl.ds(key_row, tile), :] = gk
        gv_s[pl.ds(key_row, tile), :] = gv

    @pl.loop(0, slots, unroll=8)
    def _(slot):
        row = pl.multiple_of(perm_ref[0, slot] * BLK, BLK)
        pre = x_ref[slot][:, : 3 * DH].astype(jnp.float32)
        sigma = sigmoid(pre)
        slope = sigma * (1.0 + pre * (1.0 - sigma))
        gq = gq_s[:, pl.ds(row, BLK)].T * 0.0625
        gk = gk_s[pl.ds(row, BLK), :]
        gv = gv_s[pl.ds(row, BLK), :]
        out_ref[slot, :DH, :] = (gq * slope[:, :DH]).T.astype(jnp.bfloat16)
        out_ref[slot, DH : 2 * DH, :] = (gk * slope[:, DH : 2 * DH]).T.astype(jnp.bfloat16)
        out_ref[slot, 2 * DH :, :] = (gv * slope[:, 2 * DH :]).T.astype(jnp.bfloat16)


def attention(packed, lengths, perm, tile=256):
    slots = packed.shape[0]
    whole = slots * BLK
    vmem = pl.BlockSpec(memory_space=pltpu.VMEM)
    hbm = pl.BlockSpec(memory_space=pltpu.HBM)
    lengths, perm = (pltpu.with_memory_space_constraint(array, pltpu.HBM) for array in (lengths, perm))
    bf, f32 = jnp.bfloat16, jnp.float32
    return pl.pallas_call(
        functools.partial(attention_kernel, tile),
        out_shape=jax.ShapeDtypeStruct((slots, 3 * DH, BLK), bf),
        in_specs=[hbm, hbm, vmem],
        out_specs=vmem,
        scratch_shapes=[
            pltpu.VMEM((whole, DH), bf),
            pltpu.VMEM((whole, DH), bf),
            pltpu.VMEM((whole, DH), bf),
            pltpu.VMEM((whole, DH), bf),
            pltpu.VMEM((DH, whole), bf),
            pltpu.VMEM((DH, whole), f32),
            pltpu.VMEM((whole, DH), f32),
            pltpu.VMEM((whole, DH), f32),
            pltpu.VMEM((whole // tile, tile), jnp.int32),
            pltpu.VMEM((whole // tile, tile), f32),
            pltpu.SMEM(lengths.shape, jnp.int32),
            pltpu.SMEM(perm.shape, jnp.int32),
            pltpu.SemaphoreType.DMA((2,)),
        ],
        compiler_params=pltpu.CompilerParams(vmem_limit_bytes=24 << 20),
    )(lengths, perm, packed)


class Links:
    def __init__(self, send_sem, recv_sem):
        self.send_sem, self.recv_sem = send_sem, recv_sem
        self.copies = []

    def start(self, src, dst, device):
        k = len(self.copies)
        copy = pltpu.make_async_remote_copy(
            src_ref=src,
            dst_ref=dst,
            send_sem=self.send_sem.at[k],
            recv_sem=self.recv_sem.at[k],
            device_id=device,
            device_id_type=MESH,
        )
        copy.start()
        self.copies.append(copy)
        return copy

    def wait_sends(self):
        for copy in self.copies:
            copy.wait_send()


def far_first(n):
    order = []
    for near in range(n // 2, 0, -1):
        order += sorted({near, n - near})
    return order


def all_to_all_start(links, axis, me, n, src_ref, dst_ref):
    copies = []
    for step in far_first(n):
        peer = lax.rem(me + step, n)
        copies.append(links.start(src_ref.at[peer], dst_ref.at[me], {axis: peer}))
    return copies


def plane_gather(links, own_ref, all_ref, side=4):
    dp = lax.axis_index("dp")
    core = lax.rem(dp, 2)
    chip = lax.div(dp, 2)
    x, y = lax.rem(chip, side), lax.div(chip, side)
    a = x * (1 - core) + y * core
    b = y * (1 - core) + x * core
    partner = {"dp": dp + 1 - 2 * core}
    depth = own_ref.shape[0] // 2
    part = [pl.ds(0, depth), pl.ds(depth, depth)]

    def index(i, j):
        p, q = lax.rem(a + i + side, side), lax.rem(b + j + side, side)
        px = p * (1 - core) + q * core
        py = q * (1 - core) + p * core
        return (py * side + px) * 2 + core

    def device(i, j):
        return {"dp": index(i, j)}

    across = []

    def hand_over(i, j, src=None):
        ref = all_ref.at[index(i, j)]
        across.append(links.start(ref if src is None else src, ref, partner))

    def spread(i, src=None):
        ref = all_ref.at[index(i, 0)]
        src = ref if src is None else src
        up = links.start(src, ref, device(0, 1))
        down = links.start(src, ref, device(0, -1))
        hand_over(i, 0, src)
        return up, down

    def pass_on(i, pair):
        up, down = pair
        up.wait_recv()
        ref = all_ref.at[index(i, -1), part[1]]
        far_up = links.start(ref, ref, device(0, 1))
        hand_over(i, -1)
        down.wait_recv()
        ref = all_ref.at[index(i, 1), part[0]]
        far_down = links.start(ref, ref, device(0, -1))
        hand_over(i, 1)
        return far_up, far_down

    def finish(i, pair):
        pair[0].wait_recv()
        pair[1].wait_recv()
        hand_over(i, 2)

    own_slot = all_ref.at[index(0, 0)]
    up = links.start(own_ref, own_slot, device(1, 0))
    down = links.start(own_ref, own_slot, device(-1, 0))
    first = spread(0, own_ref)
    yield
    up.wait_recv()
    ref = all_ref.at[index(-1, 0), part[1]]
    far_up = links.start(ref, ref, device(1, 0))
    second = spread(-1)
    yield
    down.wait_recv()
    ref = all_ref.at[index(1, 0), part[0]]
    far_down = links.start(ref, ref, device(-1, 0))
    third = spread(1)
    yield
    first = pass_on(0, first)
    yield
    far_up.wait_recv()
    far_down.wait_recv()
    fourth = spread(2)
    yield
    second = pass_on(-1, second)
    yield
    third = pass_on(1, third)
    yield
    finish(0, first)
    fourth = pass_on(2, fourth)
    yield
    finish(-1, second)
    finish(1, third)
    yield
    finish(2, fourth)
    yield
    for copy in across:
        copy.wait_recv()


PLANE_COPIES = 2 + 2 + 4 * 4 + 16


def greet(axis_peers):
    barrier = pltpu.get_barrier_semaphore()
    for device in axis_peers:
        pl.semaphore_signal(barrier, inc=1, device_id=device, device_id_type=MESH)
    return barrier, len(axis_peers)


def ring_peers(me, n):
    return [{"ctx": lax.rem(me + step, n)} for step in range(1, n)]


def plane_peers(dp, planes):
    return [{"dp": lax.rem(dp + step, planes)} for step in range(1, planes)]


def gather_kernel(
    n, pre_hbm, grad_hbm, tokens_ref, w_ref, recv_ref, tokens_all_ref, w_rows_ref,
    packed_ref, pre_ref, grad_ref, send_sem, recv_sem, local_sem,
):
    me = lax.axis_index("ctx")
    dp = lax.axis_index("dp")
    core = lax.rem(dp, 2)
    chip = lax.div(dp, 2)
    x, y = lax.rem(chip, 4), lax.div(chip, 4)
    peers = ring_peers(me, n)
    peers += [{"dp": dp + 1 - 2 * core}]
    peers += [{"dp": (y * 4 + lax.rem(x + step, 4)) * 2 + core} for step in (1, 3)]
    peers += [{"dp": (lax.rem(y + step, 4) * 4 + x) * 2 + core} for step in (1, 3)]
    barrier, count = greet(peers)
    links = Links(send_sem, recv_sem)
    loads = [
        pltpu.make_async_copy(pre_hbm, pre_ref, local_sem.at[3]),
        pltpu.make_async_copy(grad_hbm, grad_ref, local_sem.at[4]),
    ]
    for copy in loads:
        copy.start()
    columns = 3 * DH
    for copy in loads:
        copy.wait()
    for head in range(n):
        packed_ref[head, :, :columns] = pre_ref[:, head * columns : (head + 1) * columns]
        packed_ref[head, :, columns:] = grad_ref[:, head * DH : (head + 1) * DH]
    own = [
        pltpu.make_async_copy(tokens_ref, tokens_all_ref.at[dp], local_sem.at[1]),
        pltpu.make_async_copy(w_ref, w_rows_ref.at[me], local_sem.at[2]),
    ]
    for copy in own:
        copy.start()
    pl.semaphore_wait(barrier, count)
    own.append(pltpu.make_async_copy(packed_ref.at[me], recv_ref.at[me], local_sem.at[0]))
    own[-1].start()
    plane = plane_gather(links, tokens_ref, tokens_all_ref)
    next(plane)
    copies = all_to_all_start(links, "ctx", me, n, packed_ref, recv_ref)
    for step in far_first(n):
        copies.append(links.start(w_ref, w_rows_ref.at[me], {"ctx": lax.rem(me + step, n)}))
    for _ in plane:
        pass
    for copy in copies:
        copy.wait_recv()
    links.wait_sends()
    for copy in own:
        copy.wait()


def gather(pre, grads, tokens, w, n, planes):
    copies = (n - 1) * 2 + PLANE_COPIES
    packed = (n, tokens.shape[0], 4 * DH)
    return pl.pallas_call(
        functools.partial(gather_kernel, n),
        out_shape=(
            jax.ShapeDtypeStruct(packed, pre.dtype),
            jax.ShapeDtypeStruct((planes,) + tokens.shape, tokens.dtype),
            jax.ShapeDtypeStruct((n,) + w.shape, w.dtype),
        ),
        in_specs=[HBM, HBM, HBM, HBM],
        out_specs=(VMEM, VMEM, VMEM),
        scratch_shapes=[
            pltpu.VMEM(packed, pre.dtype),
            pltpu.VMEM(pre.shape, pre.dtype),
            pltpu.VMEM(grads.shape, grads.dtype),
            pltpu.SemaphoreType.DMA((copies,)),
            pltpu.SemaphoreType.DMA((copies,)),
            pltpu.SemaphoreType.DMA((5,)),
        ],
        compiler_params=pltpu.CompilerParams(
            collective_id=1, has_side_effects=True, vmem_limit_bytes=24 << 20
        ),
    )(*(pltpu.with_memory_space_constraint(array, pltpu.HBM) for array in (pre, grads, tokens, w)))


def push(pending, src, dst, send_sem, recv_sem, device, here):
    def remote():
        return pltpu.make_async_remote_copy(
            src_ref=src,
            dst_ref=dst,
            send_sem=send_sem,
            recv_sem=recv_sem,
            device_id=device,
            device_id_type=MESH,
        )

    @pl.when(jnp.logical_not(here))
    def _():
        remote().start()

    @pl.when(here)
    def _():
        pltpu.make_async_copy(src, dst, recv_sem).start()

    pending.append((here, remote))


def landed(ref, sem):
    pltpu.make_async_copy(ref, ref, sem).wait()


def return_kernel(
    n, planes, grad_ref, w_rows_ref, tokens_ref, input_ref, weight_ref,
    back, cols, w_all, input_sum, weight_sum, parts, rows_in, heads_in, send_sem, recv_sem,
    forward_send, forward_recv, local_sem,
):
    me = lax.axis_index("ctx")
    dp = lax.axis_index("dp")
    half = cols.shape[1]
    barrier, count = greet(ring_peers(me, n) + plane_peers(dp, planes))
    own_block = pltpu.make_async_copy(grad_ref.at[me], back.at[me], local_sem.at[0])
    own_block.start()
    own_rows = pltpu.make_async_copy(w_rows_ref, w_all.at[dp], local_sem.at[1])
    own_rows.start()
    input_sum[...] = jnp.zeros_like(input_sum)
    weight_sum[...] = jnp.zeros_like(weight_sum)
    pl.semaphore_wait(barrier, count)
    links = Links(send_sem, recv_sem)
    turn = lax.rem(lax.div(dp, 2), n - 1)
    arrivals = []
    for place in range(n - 1):
        index = lax.rem(turn + place, n - 1)
        odd, near = lax.rem(index, 2), lax.div(index, 2)
        step = (near + 1) * (1 - odd) + (n - 1 - near) * odd
        peer = lax.rem(me + step, n)
        copy = links.start(grad_ref.at[peer], back.at[me], {"ctx": peer})
        arrivals.append((lax.rem(me + n - step, n), copy))

    def forward(head, place, source):
        for side in range(2):
            owner = head * 2 + side
            push(
                pending, source.at[head, pl.ds(side * half, half)], cols.at[dp],
                forward_send.at[2 * place + side], forward_recv.at[dp], {"dp": owner}, owner == dp,
            )

    def add_head(head, carry):
        block = w_all[:, pl.ds(head, 1)].reshape(input_sum.shape[0], w_all.shape[3])
        term = jnp.dot(block, back[head], preferred_element_type=jnp.float32)
        input_sum[...] += term.astype(jnp.bfloat16).astype(jnp.float32)
        return carry

    ahead = lax.rem(me + n - lax.div(dp, 2), n)
    short = lax.div(n + n // 2 - ahead, n)
    own_place = short * 2 * (ahead - 1) + (1 - short) * (2 * n - 1 - 2 * ahead)

    def add_sources(first):
        sources = []
        for place in range(first, first + 2):
            chip = n - 1 if place == n - 1 else lax.rem(own_place - place + 2 * n - 2, n - 1)
            sources += [2 * chip, 2 * chip + 1]
        for source in sources:
            landed(cols.at[source], forward_recv.at[source])
        left = jnp.concatenate([cols[source] for source in sources], axis=1)
        right = jnp.concatenate([tokens_ref[source] for source in sources], axis=0)
        weight_sum[...] += jnp.dot(left, right, preferred_element_type=jnp.float32)

    pending = []
    forward(me, n - 1, grad_ref)
    plane = plane_gather(links, w_rows_ref, w_all)
    for _ in range(5):
        next(plane, None)
    added = 0
    for place, (head, copy) in enumerate(arrivals):
        copy.wait_recv()
        forward(head, place, back)
        next(plane, None)
        if place >= added + LAG and added + 1 < n:
            add_sources(added)
            added += 2
    own_block.wait()
    while added < n:
        add_sources(added)
        added += 2

    mean = weight_sum[...] * (1.0 / planes)
    parts[...] = mean.T.astype(parts.dtype).reshape(parts.shape)
    next(plane, None)
    own_part = pltpu.make_async_copy(parts.at[dp], rows_in.at[dp], local_sem.at[0])
    own_part.start()
    copies = all_to_all_start(links, "dp", dp, planes, parts, rows_in)
    for _ in plane:
        pass
    own_rows.wait()
    lax.fori_loop(0, 8, add_head, 0)
    own_part.wait()
    for copy in copies:
        copy.wait_recv()

    def head_rows(owner):
        return rows_in.at[pl.ds(owner * 2, 2)]

    own_head = pltpu.make_async_copy(head_rows(me), heads_in.at[me], local_sem.at[1])
    own_head.start()
    copies = []
    for step in far_first(n):
        owner = lax.rem(me + step, n)
        copies.append(links.start(head_rows(owner), heads_in.at[me], {"ctx": owner}))
    lax.fori_loop(8, n, add_head, 0)
    input_ref[...] = input_sum[...].T.astype(input_ref.dtype)
    own_head.wait()
    for copy in copies:
        copy.wait_recv()
    total = jnp.zeros(heads_in.shape[1:], jnp.float32)
    for source in range(n):
        total = total + heads_in[source].astype(jnp.float32)
    weight_ref[:, :half] = total[0]
    weight_ref[:, half:] = total[1]
    links.wait_sends()
    for here, remote in pending:

        @pl.when(jnp.logical_not(here))
        def _():
            remote().wait_send()


def send_back(grad_t, w_rows, tokens_all):
    n, columns, tokens = grad_t.shape
    planes, _, width = tokens_all.shape
    rows, half = width // planes, n * columns // planes
    copies = 2 * (n - 1) + planes - 1 + PLANE_COPIES
    bf, f32 = jnp.bfloat16, jnp.float32
    return pl.pallas_call(
        functools.partial(return_kernel, n, planes),
        out_shape=(
            jax.ShapeDtypeStruct((tokens, width), bf),
            jax.ShapeDtypeStruct((rows, columns), f32),
        ),
        in_specs=[VMEM, VMEM, VMEM],
        out_specs=(VMEM, VMEM),
        scratch_shapes=[
            pltpu.VMEM(grad_t.shape, bf),
            pltpu.VMEM((planes, half, tokens), bf),
            pltpu.VMEM((planes,) + w_rows.shape, bf),
            pltpu.VMEM((width, tokens), f32),
            pltpu.VMEM((half, width), f32),
            pltpu.VMEM((planes, rows, half), bf),
            pltpu.VMEM((planes, rows, half), bf),
            pltpu.VMEM((n, planes // n, rows, half), bf),
            pltpu.SemaphoreType.DMA((copies,)),
            pltpu.SemaphoreType.DMA((copies,)),
            pltpu.SemaphoreType.DMA((2 * n,)),
            pltpu.SemaphoreType.DMA((planes,)),
            pltpu.SemaphoreType.DMA((2,)),
        ],
        compiler_params=pltpu.CompilerParams(
            collective_id=2, has_side_effects=True, vmem_limit_bytes=36 << 20
        ),
    )(grad_t, w_rows, tokens_all)


def body(layer_input, projected, grad_output, w_qkv, lengths, block_perm):
    ctx_count = lax.axis_size("ctx")
    data_count = lax.axis_size("dp")
    blocks, tokens_all, w_rows = gather(
        projected[0], grad_output[0], layer_input[0], w_qkv, ctx_count, data_count
    )
    grad_t = attention(blocks, lengths, block_perm)
    grad_input, grad_weight = send_back(grad_t, w_rows, tokens_all)
    return (grad_input[None], grad_weight)


def solution(mesh):
    return jax.shard_map(
        body,
        mesh=mesh,
        in_specs=(
            P("dp", "ctx", None),
            P("dp", "ctx", None),
            P("dp", "ctx", None),
            P("dp", "ctx"),
            P("dp", None),
            P("dp", None),
        ),
        out_specs=(P("dp", "ctx", None), P("dp", "ctx")),
        check_vma=False,
    )
```
